128 devices in a mesh: row: 4 (over z), col: 32 (over x, y, core).
Axes of the slice: x: 4, y: 4, z: 4, core: 2. Of those that a mesh axis runs over, the one named last changes fastest.
Arguments:
- queries: bfloat16 [1024, 4096], P(('row', 'col')), may hold values from -8 to 8
- passages: bfloat16 [65536, 4096], P(('row', 'col')), may hold values from -8 to 8
- adapter: bfloat16 [4096, 768], replicated, may hold values from -0.09375 to 0.09375
- positives: int32 [1024], replicated, may hold values from 0 to 65535
Outputs:
- adapter_grad: float32 [4096, 768], P(('row', 'col'))
- query_grad: bfloat16 [1024, 4096], P(('row', 'col'))
- losses: float32 [1024], P(('row', 'col'))
The draws below stay inside these ranges and needn't reach their ends.
All inputs are finite; a program needn't handle non-finite values.
Results may differ from the reference program's by a relative error of at most 0.0088.
Values may be sent and summed in bfloat16 or wider, within the bound.
No kernel may reach another device: no remote copies, remote signals or barrier semaphores. Data moves between devices by JAX's collectives and lax.ppermute only.
A program may use at most 128 MiB of HBM per device.

```python
import jax
import jax.numpy as jnp
from jax import lax

DIN = 4096
E = 768
PASS_DEV = 512
QUERIES = 1024
PASSAGES = 65536


def cluster_centres(key):
    inner = jax.random.fold_in(key, 5)
    return jax.random.normal(jax.random.fold_in(inner, 1), (256, DIN), jnp.float32)


def cluster_shift(key, salt, count):
    centres = cluster_centres(key)
    labels = jax.random.randint(jax.random.fold_in(jax.random.fold_in(key, 6), salt), (count,), 0, 256)
    return 0.5 * centres[labels]


def draw_queries(key, part):
    shift = cluster_shift(key, 1, QUERIES)
    noise = jax.random.normal(jax.random.fold_in(key, 22), (QUERIES, DIN), jnp.float32)
    values = jnp.clip(shift + 0.87 * noise, -8.0, 8.0)
    return values.astype(jnp.bfloat16)


def draw_passages(key, part):
    shift = cluster_shift(key, 2, PASSAGES)
    noise = jax.random.normal(jax.random.fold_in(key, 32), (PASSAGES, DIN), jnp.float32)
    values = jnp.clip(shift + 0.87 * noise, -8.0, 8.0)
    return values.astype(jnp.bfloat16)


def plant(values, own_key, least, largest):
    longest = values.shape.index(max(values.shape))
    spots = []
    for shift in (0, 1):
        where = [jax.random.randint(jax.random.fold_in(own_key, axis), (), 0, length) for axis, length in enumerate(values.shape)]
        where[longest] = (where[longest] + shift) % values.shape[longest]
        spots.append(tuple(where))
    return values.at[spots[0]].set(least).at[spots[1]].set(largest)


def bell_draw(stream_key, dims, scale, most, held_as=jnp.bfloat16):
    drawn = jax.random.normal(stream_key, dims, jnp.float32) * scale
    return jnp.minimum(jnp.maximum(drawn, -most), most).astype(held_as)


def setup_inputs(seed: int = 0) -> dict:
    streams_of = jax.random.split(jax.random.key(seed), 5)
    queries = draw_queries(jax.random.fold_in(streams_of[4], 71), 0)
    passages = draw_passages(jax.random.fold_in(streams_of[4], 71), 0)
    adapter = bell_draw(streams_of[2], (DIN, E), DIN ** -0.5, 0.09375)
    positives = plant(jax.random.randint(streams_of[3], (QUERIES,), 0, PASSAGES), jax.random.fold_in(streams_of[3], 1), 0, PASSAGES - 1).astype(jnp.int32)
    return {"queries": queries, "passages": passages, "adapter": adapter, "positives": positives}


def reference(queries, passages, adapter, positives):
    scale = adapter.shape[1] ** -0.5
    width = queries.shape[1]
    qa = jnp.dot(queries, adapter, preferred_element_type=jnp.float32).astype(jnp.bfloat16)
    slabs = passages.reshape(-1, PASS_DEV, width)
    count = slabs.shape[0]
    nquery = queries.shape[0]

    def score(pa, index):
        values = jnp.dot(qa, pa.T, preferred_element_type=jnp.float32) * scale
        columns = index * PASS_DEV + jnp.arange(PASS_DEV, dtype=jnp.int32)
        return values, positives[:, None] == columns[None, :]

    def first(carry, item):
        top, total, picked = carry
        slab, index = item
        pa = jnp.dot(slab, adapter, preferred_element_type=jnp.float32).astype(jnp.bfloat16)
        values, hit = score(pa, index)
        newtop = jnp.maximum(top, jnp.max(values, axis=1))
        total = total * jnp.exp(top - newtop) + jnp.sum(jnp.exp(values - newtop[:, None]), axis=1)
        picked = picked + jnp.sum(jnp.where(hit, values, 0.0), axis=1)
        return (newtop, total, picked), pa

    start = (jnp.full((nquery,), -jnp.inf, jnp.float32), jnp.zeros((nquery,), jnp.float32), jnp.zeros((nquery,), jnp.float32))
    indices = jnp.arange(count, dtype=jnp.int32)
    (top, total, picked), projected = lax.scan(first, start, (slabs, indices))
    lse = top + jnp.log(total)

    def second(carry, item):
        dqa, dweight = carry
        slab, pa, index = item
        values, hit = score(pa, index)
        probs = jnp.exp(values - lse[:, None])
        dscores = ((probs - hit.astype(jnp.float32)) * scale).astype(jnp.bfloat16)
        dqa = dqa + jnp.dot(dscores, pa, preferred_element_type=jnp.float32)
        dpa = jnp.dot(dscores.T, qa, preferred_element_type=jnp.float32).astype(jnp.bfloat16)
        dweight = dweight + jnp.dot(slab.T, dpa, preferred_element_type=jnp.float32)
        return (dqa, dweight), None

    init = (jnp.zeros((nquery, adapter.shape[1]), jnp.float32), jnp.zeros(adapter.shape, jnp.float32))
    (dqa, dweight), unused = lax.scan(second, init, (slabs, projected, indices))
    dqa_low = dqa.astype(jnp.bfloat16)
    dweight = dweight + jnp.dot(queries.T, dqa_low, preferred_element_type=jnp.float32)
    query_grad = jnp.dot(dqa_low, adapter.T, preferred_element_type=jnp.float32).astype(jnp.bfloat16)
    return dweight, query_grad, lse - picked
```

```python
import jax
import jax.numpy as jnp
from jax import lax
from jax.sharding import Mesh
from jax.sharding import PartitionSpec as P

CHIP = ("row", "col_0", "col_1")
CORE = "col_2"
ALL = (*CHIP, CORE)
SWAP = [(0, 1), (1, 0)]
F32 = jnp.float32
BF16 = jnp.bfloat16


def dot(left, right, dims):
    return lax.dot_general(left, right, (dims, ((), ())), preferred_element_type=F32)


def to_partner(x):
    return lax.ppermute(x, CORE, SWAP)


def exchanged(blocks):
    return lax.all_to_all(blocks, CHIP, split_axis=0, concat_axis=0, tiled=True)


def logsumexp0(x):
    top = jnp.max(x, axis=0)
    return top + jnp.log(jnp.sum(jnp.exp(x - top[None]), axis=0))


def per_device(queries, passages, adapter, positives):
    width = adapter.shape[1]
    scale = width ** (-0.5)
    din = adapter.shape[0]
    own_rows, slab_rows = queries.shape[0], passages.shape[0]
    chips = lax.axis_size(CHIP)
    half = chips * own_rows
    chip, core = lax.axis_index(CHIP), lax.axis_index(CORE)
    here = chip * 2 + core

    local_qa = dot(queries, adapter, ((1,), (0,))).astype(BF16)
    qa = exchanged(jnp.broadcast_to(local_qa[None], (chips, own_rows, width)))
    qa = qa.reshape(half, width)
    pa = dot(passages, adapter, ((1,), (0,))).astype(BF16)
    pa = jnp.concatenate([pa, to_partner(pa)], axis=0)
    partner_queries = to_partner(queries)

    scores = dot(qa, pa, ((1,), (1,))) * scale
    offsets = jnp.arange(slab_rows, dtype=jnp.int32)
    columns = jnp.concatenate([here * slab_rows + offsets, (here ^ 1) * slab_rows + offsets])
    wanted = lax.dynamic_index_in_dim(
        positives.reshape(chips, 2, own_rows), core, 1, keepdims=False
    ).reshape(half)
    hit = wanted[:, None] == columns[None, :]
    top = jnp.max(scores, axis=1)
    total = jnp.sum(jnp.exp(scores - top[:, None]), axis=1)
    picked = jnp.sum(jnp.where(hit, scores, 0.0), axis=1)
    local_lse = top + jnp.log(total)
    packet = jnp.concatenate(
        [
            jnp.broadcast_to(local_lse.reshape(1, half // 128, 128), (chips, half // 128, 128)),
            jnp.pad(picked.reshape(chips, 1, own_rows), ((0, 0), (0, 0), (0, 128 - own_rows))),
        ],
        axis=1,
    )
    packet = exchanged(packet)
    lse = logsumexp0(packet[:, :-1].reshape(chips, half))
    own_picked = jnp.sum(packet[:, -1, :own_rows], axis=0)
    own_lse = lax.dynamic_slice_in_dim(lse, chip * own_rows, own_rows, 0)
    losses = own_lse - own_picked

    probs = jnp.exp(scores - lse[:, None])
    dscores = ((probs - hit.astype(F32)) * scale).astype(BF16)
    dqa = dot(dscores, pa, ((1,), (0,))).astype(BF16)
    dqa_own = exchanged(dqa.reshape(chips, own_rows, width))
    dqa_own = jnp.sum(dqa_own.astype(F32), axis=0).astype(BF16)

    dpa = dot(dscores, qa, ((0,), (0,)))
    dpa = (dpa[:slab_rows] + to_partner(dpa[slab_rows:].astype(BF16)).astype(F32)).astype(BF16)
    grad = dot(passages, dpa, ((0,), (0,))).astype(BF16).reshape(chips, 2, din // chips // 2, width)
    kept = lax.dynamic_index_in_dim(grad, core, 1, keepdims=False)
    given = lax.dynamic_index_in_dim(grad, 1 - core, 1, keepdims=False)
    given = to_partner(given)

    chip_queries = jnp.concatenate([queries, partner_queries], axis=0)
    chip_queries = lax.dynamic_index_in_dim(
        chip_queries.reshape(2 * own_rows, chips, 2, din // chips // 2), core, 2, keepdims=False
    ).reshape(2 * own_rows, din // 2)
    chip_dqa = jnp.concatenate([dqa_own, to_partner(dqa_own)], axis=0)
    from_queries = dot(chip_queries, chip_dqa, ((0,), (0,))).reshape(kept.shape)
    grad = (kept.astype(F32) + given.astype(F32) + from_queries).astype(BF16)
    grad = jnp.sum(exchanged(grad).astype(F32), axis=0)

    query_grad = dot(dqa_own, adapter, ((1,), (1,))).astype(BF16)
    return (grad, query_grad, losses)


def solution(mesh):
    torus = Mesh(mesh.devices.reshape(mesh.shape["row"], 4, 4, 2), ALL)
    rows = P(ALL, None)
    return jax.shard_map(
        per_device,
        mesh=torus,
        in_specs=(rows, rows, P(), P()),
        out_specs=(rows, rows, P(ALL)),
        check_vma=False,
    )
```

```python
import itertools

import jax
import jax.numpy as jnp
from jax import lax
from jax.sharding import Mesh
from jax.sharding import PartitionSpec as P

CHIP = ("row", "col_0", "col_1")
CORE = "col_2"
ALL = (*CHIP, CORE)
SIDE = 4
SWAP = [(0, 1), (1, 0)]
HOPS = (2, 1, 3)
ROUTES = ((0, 1, 2), (1, 2, 0))
F32 = jnp.float32
BF16 = jnp.bfloat16


def dot(left, right, dims):
    return lax.dot_general(left, right, (dims, ((), ())), preferred_element_type=F32)


def to_partner(x):
    return lax.ppermute(x, CORE, SWAP)


def exchanged(blocks):
    return lax.all_to_all(blocks, CHIP, split_axis=0, concat_axis=0, tiled=True)


def number(place, core):
    return ((place[0] * SIDE + place[1]) * SIDE + place[2]) * 2 + core


def shift(stage, hops):
    pairs = []
    for *place, core in itertools.product(range(SIDE), range(SIDE), range(SIDE), range(2)):
        there = list(place)
        axis = ROUTES[core][stage]
        there[axis] = (there[axis] + hops) % SIDE
        pairs.append((number(place, core), number(there, core)))
    return pairs


def along_line(x, stage):
    return [lax.ppermute(x, ALL, shift(stage, hops)) for hops in HOPS]


def block(x, which, dim):
    size = x.shape[dim] // SIDE
    return lax.dynamic_slice_in_dim(x, which % SIDE * size, size, dim)


def dealt(x, place, stage, dim):
    sent = [
        lax.ppermute(block(x, place + hops, dim), ALL, shift(stage, hops)) for hops in HOPS
    ]
    return [block(x, place, dim), *sent]


def by_core(x, dim, core):
    dims = x.shape
    cut = x.reshape(*dims[:dim], SIDE, SIDE, SIDE, 2, -1, *dims[dim + 1 :])
    first = lax.index_in_dim(cut, 0, dim + 3, keepdims=False)
    second = lax.index_in_dim(cut, 1, dim + 3, keepdims=False)
    second = jnp.moveaxis(second, dim, dim + 2)
    half = (*dims[:dim], dims[dim] // 2, *dims[dim + 1 :])
    first, second = first.reshape(half), second.reshape(half)
    low = core == 0
    return jnp.where(low, first, second), jnp.where(low, second, first)


def logsumexp0(x):
    top = jnp.max(x, axis=0)
    return top + jnp.log(jnp.sum(jnp.exp(x - top[None]), axis=0))


def total(parts):
    first, *others = parts
    out = first.astype(F32)
    for part in others:
        out = out + part.astype(F32)
    return out


def per_device(queries, passages, adapter, positives):
    width = adapter.shape[1]
    scale = width ** (-0.5)
    own_rows, slab_rows = queries.shape[0], passages.shape[0]
    chips = lax.axis_size(CHIP)
    half = chips * own_rows
    chip, core = lax.axis_index(CHIP), lax.axis_index(CORE)
    here = chip * 2 + core
    place = [lax.axis_index(axis) for axis in CHIP]
    stops = [
        jnp.where(core == 0, place[ROUTES[0][k]], place[ROUTES[1][k]]) for k in range(3)
    ]

    with jax.named_scope("local_qa"):
        local_qa = dot(queries, adapter, ((1,), (0,))).astype(BF16)
    with jax.named_scope("gather_qa"):
        qa = exchanged(jnp.broadcast_to(local_qa[None], (chips, own_rows, width)))
        qa = qa.reshape(half, width)
    with jax.named_scope("local_pa"):
        pa = dot(passages, adapter, ((1,), (0,))).astype(BF16)
    with jax.named_scope("pair_pa"):
        pa = jnp.concatenate([pa, to_partner(pa)], axis=0)
    with jax.named_scope("turn"):
        kept, given = by_core(passages.T, 0, core)
        turned = jnp.concatenate([kept, to_partner(given)], axis=1)
    with jax.named_scope("line_queries"):
        kept, given = by_core(queries, 1, core)
        chip_queries = jnp.concatenate([kept, to_partner(given)], axis=0)
        line_queries = jnp.concatenate(dealt(chip_queries, stops[0], 0, 1), axis=0)

    with jax.named_scope("scores"):
        scores = dot(qa, pa, ((1,), (1,))) * scale
        offsets = jnp.arange(slab_rows, dtype=jnp.int32)
        columns = jnp.concatenate(
            [here * slab_rows + offsets, (here ^ 1) * slab_rows + offsets]
        )
        wanted = lax.dynamic_index_in_dim(
            positives.reshape(chips, 2, own_rows), core, 1, keepdims=False
        ).reshape(half)
        hit = wanted[:, None] == columns[None, :]
        top = jnp.max(scores, axis=1)
        mass = jnp.sum(jnp.exp(scores - top[:, None]), axis=1)
        picked = jnp.sum(jnp.where(hit, scores, 0.0), axis=1)
        local_lse = top + jnp.log(mass)
        lanes = local_lse.reshape(1, half // 128, 128)
        packet = jnp.concatenate(
            [
                jnp.broadcast_to(lanes, (chips, *lanes.shape[1:])),
                jnp.pad(
                    picked.reshape(chips, 1, own_rows), ((0, 0), (0, 0), (0, 128 - own_rows))
                ),
            ],
            axis=1,
        )
    with jax.named_scope("gather_lse"):
        packet = exchanged(packet)
    with jax.named_scope("lse"):
        lse = logsumexp0(packet[:, :-1].reshape(chips, half))
        own_picked = jnp.sum(packet[:, -1, :own_rows], axis=0)
        own_lse = lax.dynamic_slice_in_dim(lse, chip * own_rows, own_rows, 0)
        losses = own_lse - own_picked

    with jax.named_scope("dscores"):
        probs = jnp.exp(scores - lse[:, None])
        dscores = ((probs - hit.astype(F32)) * scale).astype(BF16)
    with jax.named_scope("dpa"):
        dpa = dot(dscores, qa, ((0,), (0,)))
        there = to_partner(jnp.roll(dpa, slab_rows, axis=0).astype(BF16))
        dpa = (dpa + there.astype(F32)).astype(BF16)
    with jax.named_scope("dqa"):
        dqa = dot(dscores, pa, ((1,), (0,))).astype(BF16)
        dqa = dqa.reshape(chips, own_rows, width)
    with jax.named_scope("scatter_dqa"):
        dqa_own = exchanged(dqa)
    with jax.named_scope("sum_dqa"):
        dqa_own = jnp.sum(dqa_own.astype(F32), axis=0).astype(BF16)
    with jax.named_scope("line_dqa"):
        chip_dqa = jnp.concatenate([dqa_own, to_partner(dqa_own)], axis=0)
        line_dqa = jnp.concatenate([chip_dqa, *along_line(chip_dqa, 0)], axis=0)
    with jax.named_scope("from_queries"):
        from_queries = dot(line_queries, line_dqa, ((0,), (0,)))

    with jax.named_scope("grad"):
        grad = dot(turned, dpa, ((1,), (0,))).astype(BF16)
    with jax.named_scope("stage_0"):
        grad = (total(dealt(grad, stops[0], 0, 0)) + from_queries).astype(BF16)
    with jax.named_scope("stage_1"):
        grad = total(dealt(grad, stops[1], 1, 0)).astype(BF16)
    with jax.named_scope("stage_2"):
        grad = total(dealt(grad, stops[2], 2, 0))

    with jax.named_scope("query_grad"):
        query_grad = dot(dqa_own, adapter, ((1,), (1,))).astype(BF16)
    return (grad, query_grad, losses)


def solution(mesh):
    torus = Mesh(mesh.devices.reshape(mesh.shape["row"], SIDE, SIDE, 2), ALL)
    rows = P(ALL, None)
    return jax.shard_map(
        per_device,
        mesh=torus,
        in_specs=(rows, rows, P(), P()),
        out_specs=(rows, rows, P(ALL)),
        check_vma=False,
    )
```

```python
import functools
import itertools

import jax
import jax.numpy as jnp
from jax import lax
from jax.experimental import pallas as pl
from jax.experimental.pallas import tpu as pltpu
from jax.sharding import Mesh
from jax.sharding import PartitionSpec as P

CHIP = ("row", "col_0", "col_1")
CORE = "col_2"
ALL = (*CHIP, CORE)
SIDE = 4
SWAP = [(0, 1), (1, 0)]
HOPS = (2, 1, 3)
ROUTES = ((0, 1, 2), (1, 0, 2))
F32 = jnp.float32
BF16 = jnp.bfloat16


def dot(left, right, dims):
    return lax.dot_general(left, right, (dims, ((), ())), preferred_element_type=F32)


def to_partner(x):
    return lax.ppermute(x, CORE, SWAP)


def exchanged(blocks):
    return lax.all_to_all(blocks, CHIP, split_axis=0, concat_axis=0, tiled=True)


def number(place, core):
    return ((place[0] * SIDE + place[1]) * SIDE + place[2]) * 2 + core


def shift(stage, hops):
    pairs = []
    for *place, core in itertools.product(range(SIDE), range(SIDE), range(SIDE), range(2)):
        there = list(place)
        axis = ROUTES[core][stage]
        there[axis] = (there[axis] + hops) % SIDE
        pairs.append((number(place, core), number(there, core)))
    return pairs


def block(x, which, dim):
    size = x.shape[dim] // SIDE
    return lax.dynamic_slice_in_dim(x, which % SIDE * size, size, dim)


def dealt(x, place, stage, dim):
    sent = [
        lax.ppermute(block(x, place + hops, dim), ALL, shift(stage, hops)) for hops in HOPS
    ]
    return [block(x, place, dim), *sent]


def kernel_call(body, outs, scalars, ins, *, grid=(), scratch=(), limit=16):
    room = pl.BlockSpec(memory_space=pltpu.VMEM)
    arrays, in_specs = [], []
    for entry in ins:
        array, spec = entry if isinstance(entry, tuple) else (entry, room)
        place = pltpu.VMEM if spec is room else pltpu.HBM
        arrays.append(pltpu.with_memory_space_constraint(array, place))
        in_specs.append(spec)
    shapes, out_specs = [], []
    for shape, dtype, *spec in outs:
        shapes.append((pltpu.HBM if spec else pltpu.VMEM)(shape, dtype))
        out_specs.append(spec[0] if spec else room)
    return pl.pallas_call(
        body,
        grid_spec=pltpu.PrefetchScalarGridSpec(
            num_scalar_prefetch=1,
            grid=grid,
            in_specs=in_specs,
            out_specs=out_specs,
            scratch_shapes=list(scratch),
        ),
        out_shape=shapes,
        compiler_params=pltpu.CompilerParams(vmem_limit_bytes=limit << 20),
    )(scalars, *arrays)


def turn_kernel(core_ref, passages_ref, queries_ref, kept_ref, given_ref, kept_q_ref, given_q_ref):
    low = core_ref[0] == 0
    step = pl.program_id(0)
    lanes, width = 128, passages_ref.shape[1]
    run = 32
    base = pl.multiple_of(step * (width // 2), width // 2)
    unit = (
        lax.broadcasted_iota(jnp.int32, (lanes, lanes), 0)
        == lax.broadcasted_iota(jnp.int32, (lanes, lanes), 1)
    ).astype(BF16)
    for tile in range(width // lanes):
        here = passages_ref[:, tile * lanes : (tile + 1) * lanes]
        turned = dot(unit, here, ((1,), (1,))).astype(BF16)
        for part in range(2):
            first = turned[2 * part * run : (2 * part + 1) * run]
            second = turned[(2 * part + 1) * run : (2 * part + 2) * run]
            at = (2 * tile + part) * run
            kept_ref[pl.ds(base + at, run), :] = jnp.where(low, first, second)
            given_ref[at : at + run, :] = jnp.where(low, second, first)
    line = lax.broadcasted_iota(jnp.int32, (2 * lanes, lanes), 0)
    lane = lax.broadcasted_iota(jnp.int32, (2 * lanes, lanes), 1)
    source = lane // run * (2 * run) + lane % run
    mine = core_ref[0] * run
    pick = (line == source + mine).astype(BF16)
    leave = (line == source + run - mine).astype(BF16)
    for tile in range(width // (2 * lanes)):
        here = queries_ref[:, tile * 2 * lanes : (tile + 1) * 2 * lanes]
        to = pl.ds(pl.multiple_of(base + tile * lanes, lanes), lanes)
        kept_q_ref[:, to] = dot(here, pick, ((1,), (0,))).astype(BF16)
        given_q_ref[:, to] = dot(here, leave, ((1,), (0,))).astype(BF16)


def score_kernel(scale, here_ref, qa_ref, own_ref, other_ref, wanted_ref, scores_ref, stats_ref):
    slab = own_ref.shape[0]
    qa, wanted = qa_ref[...], wanted_ref[...]
    lines = lax.broadcasted_iota(jnp.int32, (slab, qa.shape[0]), 0)
    parts = []
    for k, ref in enumerate((own_ref, other_ref)):
        part = dot(ref[...], qa, ((1,), (1,))) * scale
        scores_ref[k * slab : (k + 1) * slab, :] = part
        hit = lines == wanted - here_ref[k]
        parts.append((part, jnp.sum(jnp.where(hit, part, 0.0), axis=0, keepdims=True)))
    top = jnp.maximum(*[jnp.max(part, axis=0, keepdims=True) for part, _ in parts])
    mass = sum(jnp.sum(jnp.exp(part - top), axis=0, keepdims=True) for part, _ in parts)
    lse = top + jnp.log(mass)
    picked = parts[0][1] + parts[1][1]
    lines = qa.shape[0] // 128
    for k in range(lines):
        at = slice(k * 128, (k + 1) * 128)
        stats_ref[k : k + 1, :] = lse[:, at]
        stats_ref[lines + k : lines + k + 1, :] = picked[:, at]


def soft_kernel(scale, here_ref, scores_ref, packet_ref, wanted_ref, qa_ref, own_ref, other_ref, dpa_ref, dqa_ref, stats_ref):
    slab, count = own_ref.shape[0], qa_ref.shape[0]
    lines = count // 128
    packet = packet_ref[...]
    each = packet[:, :lines]
    top = jnp.max(each, axis=0)
    lse = top + jnp.log(jnp.sum(jnp.exp(each - top[None]), axis=0))
    stats_ref[...] = lse - jnp.sum(packet[:, lines:], axis=0)
    row = jnp.concatenate([lse[k : k + 1] for k in range(lines)], axis=1)
    wanted = wanted_ref[...]
    rank = lax.broadcasted_iota(jnp.int32, (slab, count), 0)
    dqa = None
    for k, ref in enumerate((own_ref, other_ref)):
        at = slice(k * slab, (k + 1) * slab)
        probs = jnp.exp(scores_ref[at, :] - row)
        hit = (rank == wanted - here_ref[k]).astype(F32)
        dscores = ((probs - hit) * scale).astype(BF16)
        dpa_ref[at, :] = dot(dscores, qa_ref[...], ((1,), (0,))).astype(BF16)
        part = dot(dscores, ref[...], ((0,), (0,)))
        dqa = part if dqa is None else dqa + part
    dqa_ref[...] = dqa.astype(BF16)


def grad_kernel(where_ref, kept_ref, got_ref, mine_ref, theirs_ref, *refs):
    outs, (left_ref, sum_ref, sems) = refs[:-3], refs[-3:]
    slab = kept_ref.shape[1]
    piece = kept_ref.shape[0] // (SIDE * SIDE)
    low = where_ref[0] == 0
    copies = []
    for k, hops in enumerate((*HOPS, 0)):
        place = lax.rem(where_ref[1] + hops, SIDE)
        copies.append([])
        for j in range(SIDE):
            index = jnp.where(low, place * SIDE + j, j * SIDE + place)
            rows = pl.ds(pl.multiple_of(index * piece, piece), piece)
            for half, ref in enumerate((kept_ref, got_ref)):
                to = left_ref.at[k, j * piece : (j + 1) * piece, half * slab : (half + 1) * slab]
                copies[-1].append(pltpu.make_async_copy(ref.at[rows], to, sems.at[k, 2 * j + half]))
                copies[-1][-1].start()
    for k in range(2):
        ours, yours = slice(k * slab, (k + 1) * slab), slice((1 - k) * slab, (2 - k) * slab)
        both = mine_ref[ours, :].astype(F32) + theirs_ref[yours, :].astype(F32)
        sum_ref[ours, :] = both.astype(BF16)
    for k, out in enumerate(outs):
        for copy in copies[k]:
            copy.wait()
        out[...] = dot(left_ref[k], sum_ref[...], ((1,), (0,))).astype(BF16)


def join_kernel(stop_ref, own_ref, far_ref, next_ref, last_ref, line_ref, *outs):
    size = own_ref.shape[0]
    piece = outs[0].shape[0]
    for out, hops in zip(outs, (*HOPS, 0)):
        place = lax.rem(stop_ref[0] + hops, SIDE)
        rows = pl.ds(pl.multiple_of(place * piece, piece), piece)
        lanes = pl.ds(pl.multiple_of(place * piece, piece), piece)
        part = dot(line_ref[:, lanes], line_ref[:, size:], ((0,), (0,)))
        for ref in (own_ref, far_ref, next_ref, last_ref):
            part += ref[rows, :].astype(F32)
        out[...] = part.astype(BF16)


def line_block(x, which, core):
    cut = x.reshape(x.shape[0], SIDE, SIDE, -1)
    low = lax.dynamic_index_in_dim(cut, which % SIDE, 1, keepdims=False)
    high = lax.dynamic_index_in_dim(cut, which % SIDE, 2, keepdims=False)
    return jnp.where(core == 0, low, high).reshape(x.shape[0], -1)


def total(parts):
    first, *others = parts
    out = first.astype(F32)
    for part in others:
        out = out + part.astype(F32)
    return out


def per_device(queries, passages, adapter, positives):
    width = adapter.shape[1]
    scale = width ** (-0.5)
    din = adapter.shape[0]
    own_rows, slab_rows = queries.shape[0], passages.shape[0]
    chips = lax.axis_size(CHIP)
    half = chips * own_rows
    chip, core = lax.axis_index(CHIP), lax.axis_index(CORE)
    here = chip * 2 + core
    place = [lax.axis_index(axis) for axis in CHIP]
    stops = [
        jnp.where(core == 0, place[ROUTES[0][k]], place[ROUTES[1][k]]) for k in range(3)
    ]

    parts = 8
    span = din // parts
    local_qa = dot(queries, adapter, ((1,), (0,))).astype(BF16)
    qa = exchanged(jnp.broadcast_to(local_qa[None], (chips, own_rows, width)))
    qa = qa.reshape(half, width)
    pa = dot(passages, adapter, ((1,), (0,))).astype(BF16)
    pa_other = to_partner(pa)
    kept, given, kept_queries, given_queries = kernel_call(
        turn_kernel,
        [
            ((din // 2, slab_rows), BF16),
            ((din // 2, slab_rows), BF16, pl.BlockSpec((span // 2, slab_rows), lambda i, c: (i, 0))),
            ((own_rows, din // 2), BF16),
            ((own_rows, din // 2), BF16),
        ],
        core.reshape(1),
        [
            (passages, pl.BlockSpec((slab_rows, span), lambda i, c: (0, i))),
            (queries, pl.BlockSpec((own_rows, span), lambda i, c: (0, i))),
        ],
        grid=(parts,),
    )
    got = to_partner(given)
    chip_queries = jnp.concatenate([kept_queries, to_partner(given_queries)], axis=0)

    starts = jnp.stack([here * slab_rows, (here ^ 1) * slab_rows])
    wanted = lax.dynamic_index_in_dim(
        positives.reshape(chips, 2, own_rows), core, 1, keepdims=False
    ).reshape(1, half)
    lines = half // 128
    scores, stats = kernel_call(
        functools.partial(score_kernel, scale),
        [((2 * slab_rows, half), F32), ((2 * lines, 128), F32)],
        starts,
        [qa, pa, pa_other, wanted],
    )
    packet = jnp.broadcast_to(stats[None], (chips, *stats.shape))
    packet = exchanged(packet)
    dpa, dqa, losses = kernel_call(
        functools.partial(soft_kernel, scale),
        [((2 * slab_rows, width), BF16), ((half, width), BF16), ((lines, 128), F32)],
        starts,
        [scores, packet, wanted, qa, pa, pa_other],
    )
    losses = lax.dynamic_slice_in_dim(losses.reshape(half), chip * own_rows, own_rows, 0)
    dpa_got = to_partner(dpa)
    dqa = dqa.reshape(chips, own_rows, width)
    dqa_own = exchanged(dqa)
    dqa_own = jnp.sum(dqa_own.astype(F32), axis=0).astype(BF16)
    chip_dqa = jnp.concatenate([dqa_own, to_partner(dqa_own)], axis=0)
    loads = [
        jnp.concatenate([line_block(chip_queries, stops[0] + hops, core), chip_dqa], axis=1)
        for hops in (*HOPS, 0)
    ]
    line = [lax.ppermute(x, ALL, shift(0, hops)) for x, hops in zip(loads, HOPS)]
    line = jnp.concatenate([loads[-1], *line], axis=0)

    far = pl.BlockSpec(memory_space=pltpu.HBM)
    *sent, own = kernel_call(
        grad_kernel,
        [((kept.shape[0] // SIDE, width), BF16)] * SIDE,
        jnp.stack([core, stops[0]]),
        [(kept, far), (got, far), dpa, dpa_got],
        scratch=[
            pltpu.VMEM((SIDE, kept.shape[0] // SIDE, 2 * slab_rows), BF16),
            pltpu.VMEM(dpa.shape, BF16),
            pltpu.SemaphoreType.DMA((SIDE, 2 * SIDE)),
        ],
    )
    sent = [lax.ppermute(x, ALL, shift(0, hops)) for x, hops in zip(sent, HOPS)]
    *sent, own = kernel_call(
        join_kernel,
        [((own.shape[0] // SIDE, width), BF16)] * SIDE,
        stops[1].reshape(1),
        [own, *sent, line],
    )
    sent = [lax.ppermute(x, ALL, shift(1, hops)) for x, hops in zip(sent, HOPS)]
    grad = total([own, *sent]).astype(BF16)
    grad = total(dealt(grad, stops[2], 2, 0))

    query_grad = dot(dqa_own, adapter, ((1,), (1,))).astype(BF16)
    return (grad, query_grad, losses)


def solution(mesh):
    torus = Mesh(mesh.devices.reshape(mesh.shape["row"], SIDE, SIDE, 2), ALL)
    rows = P(ALL, None)
    return jax.shard_map(
        per_device,
        mesh=torus,
        in_specs=(rows, rows, P(), P()),
        out_specs=(rows, rows, P(ALL)),
        check_vma=False,
    )
```

```python
import functools
import itertools

import jax
import jax.numpy as jnp
from jax import lax
from jax.experimental import pallas as pl
from jax.experimental.pallas import tpu as pltpu
from jax.sharding import Mesh
from jax.sharding import PartitionSpec as P

CHIP = ("row", "col_0", "col_1")
CORE = "col_2"
ALL = (*CHIP, CORE)
SIDE = 4
SWAP = [(0, 1), (1, 0)]
HOPS = (2, 1, 3)
ROUTES = ((0, 1, 2), (1, 0, 2))
F32 = jnp.float32
BF16 = jnp.bfloat16


def dot(left, right, dims):
    return lax.dot_general(left, right, (dims, ((), ())), preferred_element_type=F32)


def to_partner(x):
    return lax.ppermute(x, CORE, SWAP)


def exchanged(blocks):
    return lax.all_to_all(blocks, CHIP, split_axis=0, concat_axis=0, tiled=True)


def number(place, core):
    return ((place[0] * SIDE + place[1]) * SIDE + place[2]) * 2 + core


def shift(stage, hops):
    pairs = []
    for *place, core in itertools.product(range(SIDE), range(SIDE), range(SIDE), range(2)):
        there = list(place)
        axis = ROUTES[core][stage]
        there[axis] = (there[axis] + hops) % SIDE
        pairs.append((number(place, core), number(there, core)))
    return pairs


def block(x, which, dim):
    size = x.shape[dim] // SIDE
    return lax.dynamic_slice_in_dim(x, which % SIDE * size, size, dim)


def dealt(x, place, stage, dim):
    sent = [
        lax.ppermute(block(x, place + hops, dim), ALL, shift(stage, hops)) for hops in HOPS
    ]
    return [block(x, place, dim), *sent]


def kernel_call(body, outs, scalars, ins, *, grid=(), scratch=(), limit=16):
    room = pl.BlockSpec(memory_space=pltpu.VMEM)
    arrays, in_specs = [], []
    for entry in ins:
        array, spec = entry if isinstance(entry, tuple) else (entry, room)
        place = pltpu.VMEM if spec is room else pltpu.HBM
        arrays.append(pltpu.with_memory_space_constraint(array, place))
        in_specs.append(spec)
    shapes, out_specs = [], []
    for shape, dtype, *spec in outs:
        shapes.append((pltpu.HBM if spec else pltpu.VMEM)(shape, dtype))
        out_specs.append(spec[0] if spec else room)
    return pl.pallas_call(
        body,
        grid_spec=pltpu.PrefetchScalarGridSpec(
            num_scalar_prefetch=1,
            grid=grid,
            in_specs=in_specs,
            out_specs=out_specs,
            scratch_shapes=list(scratch),
        ),
        out_shape=shapes,
        compiler_params=pltpu.CompilerParams(vmem_limit_bytes=limit << 20),
    )(scalars, *arrays)


def main_kernel(
    core_ref, passages_ref, adapter_ref, queries_ref,
    pa_ref, kept_ref, given_ref, kept_q_ref, given_q_ref,
    slab_ref, held_ref, turned_ref, acc_ref, in_sems, out_sems,
):
    low = core_ref[0] == 0
    parts = in_sems.shape[1]
    span = slab_ref.shape[1] // parts
    lanes, run = 128, 32
    arrivals, leaving = [], []
    for k in range(parts):
        at = slice(k * span, (k + 1) * span)
        arrivals.append(
            (
                pltpu.make_async_copy(passages_ref.at[:, at], slab_ref.at[:, at], in_sems.at[0, k]),
                pltpu.make_async_copy(adapter_ref.at[at], held_ref.at[at], in_sems.at[1, k]),
            )
        )
    for copy in itertools.chain(*arrivals):
        copy.start()
    line = lax.broadcasted_iota(jnp.int32, (2 * lanes, lanes), 0)
    lane = lax.broadcasted_iota(jnp.int32, (2 * lanes, lanes), 1)
    source = lane // run * (2 * run) + lane % run
    mine = core_ref[0] * run
    pick = (line == source + mine).astype(BF16)
    leave = (line == source + run - mine).astype(BF16)
    for tile in range(queries_ref.shape[1] // (2 * lanes)):
        here = queries_ref[:, tile * 2 * lanes : (tile + 1) * 2 * lanes]
        to = slice(tile * lanes, (tile + 1) * lanes)
        kept_q_ref[:, to] = dot(here, pick, ((1,), (0,))).astype(BF16)
        given_q_ref[:, to] = dot(here, leave, ((1,), (0,))).astype(BF16)
    unit = (
        lax.broadcasted_iota(jnp.int32, (lanes, lanes), 0)
        == lax.broadcasted_iota(jnp.int32, (lanes, lanes), 1)
    ).astype(BF16)
    for k in range(parts):
        at = slice(k * span, (k + 1) * span)
        arrivals[k][0].wait()
        for tile in range(k * span // lanes, (k + 1) * span // lanes):
            here = slab_ref[:, tile * lanes : (tile + 1) * lanes]
            turned = dot(unit, here, ((1,), (1,))).astype(BF16)
            for part in range(2):
                first = turned[2 * part * run : (2 * part + 1) * run]
                second = turned[(2 * part + 1) * run : (2 * part + 2) * run]
                to = slice((2 * tile + part) * run, (2 * tile + part + 1) * run)
                turned_ref[0, to, :] = jnp.where(low, first, second)
                turned_ref[1, to, :] = jnp.where(low, second, first)
        rows = slice(k * span // 2, (k + 1) * span // 2)
        for which, ref in enumerate((kept_ref, given_ref)):
            copy = pltpu.make_async_copy(
                turned_ref.at[which, rows], ref.at[rows], out_sems.at[which, k]
            )
            copy.start()
            leaving.append(copy)
        arrivals[k][1].wait()
        part = dot(slab_ref[:, at], held_ref[at, :], ((1,), (0,)))
        if k == 0:
            acc_ref[...] = part
        elif k < parts - 1:
            acc_ref[...] += part
        else:
            pa_ref[...] = (acc_ref[...] + part).astype(BF16)
    for copy in leaving:
        copy.wait()


def score_kernel(scale, here_ref, qa_ref, own_ref, other_ref, wanted_ref, scores_ref, stats_ref):
    slab = own_ref.shape[0]
    qa, wanted = qa_ref[...], wanted_ref[...]
    lines = lax.broadcasted_iota(jnp.int32, (slab, qa.shape[0]), 0)
    parts = []
    for k, ref in enumerate((own_ref, other_ref)):
        part = dot(ref[...], qa, ((1,), (1,))) * scale
        scores_ref[k * slab : (k + 1) * slab, :] = part
        hit = lines == wanted - here_ref[k]
        parts.append((part, jnp.sum(jnp.where(hit, part, 0.0), axis=0, keepdims=True)))
    top = jnp.maximum(*[jnp.max(part, axis=0, keepdims=True) for part, _ in parts])
    mass = sum(jnp.sum(jnp.exp(part - top), axis=0, keepdims=True) for part, _ in parts)
    lse = top + jnp.log(mass)
    picked = parts[0][1] + parts[1][1]
    lines = qa.shape[0] // 128
    for k in range(lines):
        at = slice(k * 128, (k + 1) * 128)
        stats_ref[k : k + 1, :] = lse[:, at]
        stats_ref[lines + k : lines + k + 1, :] = picked[:, at]


def soft_kernel(scale, here_ref, scores_ref, packet_ref, wanted_ref, qa_ref, own_ref, other_ref, dpa_ref, dqa_ref, stats_ref):
    slab, count = own_ref.shape[0], qa_ref.shape[0]
    lines = count // 128
    packet = packet_ref[...]
    each = packet[:, :lines]
    top = jnp.max(each, axis=0)
    lse = top + jnp.log(jnp.sum(jnp.exp(each - top[None]), axis=0))
    stats_ref[...] = lse - jnp.sum(packet[:, lines:], axis=0)
    row = jnp.concatenate([lse[k : k + 1] for k in range(lines)], axis=1)
    wanted = wanted_ref[...]
    rank = lax.broadcasted_iota(jnp.int32, (slab, count), 0)
    dqa = None
    for k, ref in enumerate((own_ref, other_ref)):
        at = slice(k * slab, (k + 1) * slab)
        probs = jnp.exp(scores_ref[at, :] - row)
        hit = (rank == wanted - here_ref[k]).astype(F32)
        dscores = ((probs - hit) * scale).astype(BF16)
        dpa_ref[at, :] = dot(dscores, qa_ref[...], ((1,), (0,))).astype(BF16)
        part = dot(dscores, ref[...], ((0,), (0,)))
        dqa = part if dqa is None else dqa + part
    dqa_ref[...] = dqa.astype(BF16)


def grad_kernel(where_ref, kept_ref, got_ref, mine_ref, theirs_ref, *refs):
    outs, (left_ref, sum_ref, sent_ref, in_sems, out_sems) = refs[:SIDE], refs[SIDE:]
    slab = kept_ref.shape[1]
    piece = kept_ref.shape[0] // (SIDE * SIDE)
    low = where_ref[0] == 0
    arrivals, leaving = [], []
    for k, hops in enumerate((*HOPS, 0)):
        place = lax.rem(where_ref[1] + hops, SIDE)
        arrivals.append([])
        for j in range(SIDE):
            index = jnp.where(low, place * SIDE + j, j * SIDE + place)
            rows = pl.ds(pl.multiple_of(index * piece, piece), piece)
            for which, ref in enumerate((kept_ref, got_ref)):
                to = left_ref.at[which, k, j * piece : (j + 1) * piece]
                copy = pltpu.make_async_copy(ref.at[rows], to, in_sems.at[k, 2 * j + which])
                arrivals[-1].append(copy)
    for copy in itertools.chain(*arrivals):
        copy.start()
    for k in range(2):
        ours, yours = slice(k * slab, (k + 1) * slab), slice((1 - k) * slab, (2 - k) * slab)
        both = mine_ref[ours, :].astype(F32) + theirs_ref[yours, :].astype(F32)
        sum_ref[ours, :] = both.astype(BF16)
    for k, out in enumerate(outs):
        for copy in arrivals[k]:
            copy.wait()
        block = dot(left_ref[0, k], sum_ref[:slab, :], ((1,), (0,)))
        block += dot(left_ref[1, k], sum_ref[slab:, :], ((1,), (0,)))
        if k < SIDE - 1:
            sent_ref[k] = block.astype(BF16)
            leaving.append(pltpu.make_async_copy(sent_ref.at[k], out, out_sems.at[k]))
            leaving[-1].start()
        else:
            out[...] = block.astype(BF16)
    for copy in leaving:
        copy.wait()


def join_kernel(stop_ref, own_ref, far_ref, next_ref, last_ref, line_ref, *outs):
    size = own_ref.shape[0]
    piece = outs[0].shape[0]
    for out, hops in zip(outs, (*HOPS, 0)):
        place = lax.rem(stop_ref[0] + hops, SIDE)
        rows = pl.ds(pl.multiple_of(place * piece, piece), piece)
        lanes = pl.ds(pl.multiple_of(place * piece, piece), piece)
        part = dot(line_ref[:, lanes], line_ref[:, size:], ((0,), (0,)))
        for ref in (own_ref, far_ref, next_ref, last_ref):
            part += ref[rows, :].astype(F32)
        out[...] = part.astype(BF16)


def line_block(x, which, core):
    cut = x.reshape(x.shape[0], SIDE, SIDE, -1)
    low = lax.dynamic_index_in_dim(cut, which % SIDE, 1, keepdims=False)
    high = lax.dynamic_index_in_dim(cut, which % SIDE, 2, keepdims=False)
    return jnp.where(core == 0, low, high).reshape(x.shape[0], -1)


def total(parts):
    first, *others = parts
    out = first.astype(F32)
    for part in others:
        out = out + part.astype(F32)
    return out


def per_device(queries, passages, adapter, positives):
    width = adapter.shape[1]
    scale = width ** (-0.5)
    din = adapter.shape[0]
    own_rows, slab_rows = queries.shape[0], passages.shape[0]
    chips = lax.axis_size(CHIP)
    half = chips * own_rows
    chip, core = lax.axis_index(CHIP), lax.axis_index(CORE)
    here = chip * 2 + core
    place = [lax.axis_index(axis) for axis in CHIP]
    stops = [
        jnp.where(core == 0, place[ROUTES[0][k]], place[ROUTES[1][k]]) for k in range(3)
    ]

    parts = 4
    far = pl.BlockSpec(memory_space=pltpu.HBM)
    dma = pltpu.SemaphoreType.DMA
    local_qa = dot(queries, adapter, ((1,), (0,))).astype(BF16)
    qa = exchanged(jnp.broadcast_to(local_qa[None], (chips, own_rows, width)))
    qa = qa.reshape(half, width)
    pa, kept, given, kept_queries, given_queries = kernel_call(
        main_kernel,
        [
            ((slab_rows, width), BF16),
            ((din // 2, slab_rows), BF16, far),
            ((din // 2, slab_rows), BF16, far),
            ((own_rows, din // 2), BF16),
            ((own_rows, din // 2), BF16),
        ],
        core.reshape(1),
        [(passages, far), (adapter, far), queries],
        scratch=[
            pltpu.VMEM((slab_rows, din), BF16),
            pltpu.VMEM((din, width), BF16),
            pltpu.VMEM((2, din // 2, slab_rows), BF16),
            pltpu.VMEM((slab_rows, width), F32),
            dma((2, parts)),
            dma((2, parts)),
        ],
        limit=28,
    )
    pa_other = to_partner(pa)
    got = to_partner(given)
    chip_queries = jnp.concatenate([kept_queries, to_partner(given_queries)], axis=0)

    starts = jnp.stack([here * slab_rows, (here ^ 1) * slab_rows])
    wanted = lax.dynamic_index_in_dim(
        positives.reshape(chips, 2, own_rows), core, 1, keepdims=False
    ).reshape(1, half)
    lines = half // 128
    scores, stats = kernel_call(
        functools.partial(score_kernel, scale),
        [((2 * slab_rows, half), F32), ((2 * lines, 128), F32)],
        starts,
        [qa, pa, pa_other, wanted],
    )
    packet = jnp.broadcast_to(stats[None], (chips, *stats.shape))
    packet = exchanged(packet)
    dpa, dqa, losses = kernel_call(
        functools.partial(soft_kernel, scale),
        [((2 * slab_rows, width), BF16), ((half, width), BF16), ((lines, 128), F32)],
        starts,
        [scores, packet, wanted, qa, pa, pa_other],
    )
    losses = lax.dynamic_slice_in_dim(losses.reshape(half), chip * own_rows, own_rows, 0)
    dpa_got = to_partner(dpa)
    dqa = dqa.reshape(chips, own_rows, width)
    dqa_own = exchanged(dqa)
    dqa_own = jnp.sum(dqa_own.astype(F32), axis=0).astype(BF16)
    chip_dqa = jnp.concatenate([dqa_own, to_partner(dqa_own)], axis=0)
    loads = [
        jnp.concatenate([line_block(chip_queries, stops[0] + hops, core), chip_dqa], axis=1)
        for hops in (*HOPS, 0)
    ]
    line = [lax.ppermute(x, ALL, shift(0, hops)) for x, hops in zip(loads, HOPS)]
    line = jnp.concatenate([loads[-1], *line], axis=0)

    block = (kept.shape[0] // SIDE, width)
    *sent, own = kernel_call(
        grad_kernel,
        [(block, BF16, far)] * len(HOPS) + [(block, BF16)],
        jnp.stack([core, stops[0]]),
        [(kept, far), (got, far), dpa, dpa_got],
        scratch=[
            pltpu.VMEM((2, SIDE, block[0], slab_rows), BF16),
            pltpu.VMEM(dpa.shape, BF16),
            pltpu.VMEM((len(HOPS), *block), BF16),
            dma((SIDE, 2 * SIDE)),
            dma((len(HOPS),)),
        ],
    )
    sent = [lax.ppermute(x, ALL, shift(0, hops)) for x, hops in zip(sent, HOPS)]
    *sent, own = kernel_call(
        join_kernel,
        [((own.shape[0] // SIDE, width), BF16)] * SIDE,
        stops[1].reshape(1),
        [own, *sent, line],
    )
    sent = [lax.ppermute(x, ALL, shift(1, hops)) for x, hops in zip(sent, HOPS)]
    grad = total([own, *sent]).astype(BF16)
    grad = total(dealt(grad, stops[2], 2, 0))

    query_grad = dot(dqa_own, adapter, ((1,), (1,))).astype(BF16)
    return (grad, query_grad, losses)


def solution(mesh):
    torus = Mesh(mesh.devices.reshape(mesh.shape["row"], SIDE, SIDE, 2), ALL)
    rows = P(ALL, None)
    return jax.shard_map(
        per_device,
        mesh=torus,
        in_specs=(rows, rows, P(), P()),
        out_specs=(rows, rows, P(ALL)),
        check_vma=False,
    )
```

```python
import functools
import itertools

import jax
import jax.numpy as jnp
from jax import lax
from jax.experimental import pallas as pl
from jax.experimental.pallas import tpu as pltpu
from jax.sharding import Mesh
from jax.sharding import PartitionSpec as P

CHIP = ("row", "col_0", "col_1")
CORE = "col_2"
ALL = (*CHIP, CORE)
SIDE = 4
SWAP = [(0, 1), (1, 0)]
HOPS = (2, 1, 3)
LINE = (0, 1)
F32 = jnp.float32
BF16 = jnp.bfloat16


def dot(left, right, dims):
    return lax.dot_general(left, right, (dims, ((), ())), preferred_element_type=F32)


def to_partner(x):
    return lax.ppermute(x, CORE, SWAP)


def exchanged(blocks):
    return lax.all_to_all(blocks, CHIP, split_axis=0, concat_axis=0, tiled=True)


def number(place, core):
    return ((place[0] * SIDE + place[1]) * SIDE + place[2]) * 2 + core


def shift(hops):
    pairs = []
    for *place, core in itertools.product(range(SIDE), range(SIDE), range(SIDE), range(2)):
        there = list(place)
        axis = LINE[core]
        there[axis] = (there[axis] + hops) % SIDE
        pairs.append((number(place, core), number(there, core)))
    return pairs


def planes():
    side = range(SIDE)
    return [
        [number((z, x, y), 0) for x in side for y in side] for z in side
    ] + [[number((z, x, y), 1) for z in side for y in side] for x in side]


def kernel_call(body, outs, scalars, ins, *, grid=(), scratch=(), limit=16):
    room = pl.BlockSpec(memory_space=pltpu.VMEM)
    arrays, in_specs = [], []
    for entry in ins:
        array, spec = entry if isinstance(entry, tuple) else (entry, room)
        place = pltpu.VMEM if spec is room else pltpu.HBM
        arrays.append(pltpu.with_memory_space_constraint(array, place))
        in_specs.append(spec)
    shapes, out_specs = [], []
    for shape, dtype, *spec in outs:
        shapes.append((pltpu.HBM if spec else pltpu.VMEM)(shape, dtype))
        out_specs.append(spec[0] if spec else room)
    return pl.pallas_call(
        body,
        grid_spec=pltpu.PrefetchScalarGridSpec(
            num_scalar_prefetch=1,
            grid=grid,
            in_specs=in_specs,
            out_specs=out_specs,
            scratch_shapes=list(scratch),
        ),
        out_shape=shapes,
        compiler_params=pltpu.CompilerParams(vmem_limit_bytes=limit << 20),
    )(scalars, *arrays)


def main_kernel(
    core_ref, passages_ref, adapter_ref, queries_ref,
    pa_ref, kept_ref, given_ref, kept_q_ref, given_q_ref,
    slab_ref, held_ref, turned_ref, acc_ref, in_sems, out_sems,
):
    low = core_ref[0] == 0
    parts = in_sems.shape[1]
    span = slab_ref.shape[1] // parts
    lanes, run = 128, 32
    arrivals, leaving = [], []
    for k in range(parts):
        at = slice(k * span, (k + 1) * span)
        arrivals.append(
            (
                pltpu.make_async_copy(passages_ref.at[:, at], slab_ref.at[:, at], in_sems.at[0, k]),
                pltpu.make_async_copy(adapter_ref.at[at], held_ref.at[at], in_sems.at[1, k]),
            )
        )
    for copy in itertools.chain(*arrivals):
        copy.start()
    line = lax.broadcasted_iota(jnp.int32, (2 * lanes, lanes), 0)
    lane = lax.broadcasted_iota(jnp.int32, (2 * lanes, lanes), 1)
    source = lane // run * (2 * run) + lane % run
    mine = core_ref[0] * run
    pick = (line == source + mine).astype(BF16)
    leave = (line == source + run - mine).astype(BF16)
    for tile in range(queries_ref.shape[1] // (2 * lanes)):
        here = queries_ref[:, tile * 2 * lanes : (tile + 1) * 2 * lanes]
        to = slice(tile * lanes, (tile + 1) * lanes)
        kept_q_ref[:, to] = dot(here, pick, ((1,), (0,))).astype(BF16)
        given_q_ref[:, to] = dot(here, leave, ((1,), (0,))).astype(BF16)
    unit = (
        lax.broadcasted_iota(jnp.int32, (lanes, lanes), 0)
        == lax.broadcasted_iota(jnp.int32, (lanes, lanes), 1)
    ).astype(BF16)
    for k in range(parts):
        at = slice(k * span, (k + 1) * span)
        arrivals[k][0].wait()
        for tile in range(k * span // lanes, (k + 1) * span // lanes):
            here = slab_ref[:, tile * lanes : (tile + 1) * lanes]
            turned = dot(unit, here, ((1,), (1,))).astype(BF16)
            for part in range(2):
                first = turned[2 * part * run : (2 * part + 1) * run]
                second = turned[(2 * part + 1) * run : (2 * part + 2) * run]
                to = slice((2 * tile + part) * run, (2 * tile + part + 1) * run)
                turned_ref[0, to, :] = jnp.where(low, first, second)
                turned_ref[1, to, :] = jnp.where(low, second, first)
        rows = slice(k * span // 2, (k + 1) * span // 2)
        for which, ref in enumerate((kept_ref, given_ref)):
            copy = pltpu.make_async_copy(
                turned_ref.at[which, rows], ref.at[rows], out_sems.at[which, k]
            )
            copy.start()
            leaving.append(copy)
        arrivals[k][1].wait()
        part = dot(slab_ref[:, at], held_ref[at, :], ((1,), (0,)))
        if k == 0:
            acc_ref[...] = part
        elif k < parts - 1:
            acc_ref[...] += part
        else:
            pa_ref[...] = (acc_ref[...] + part).astype(BF16)
    for copy in leaving:
        copy.wait()


def score_kernel(scale, here_ref, qa_ref, own_ref, other_ref, wanted_ref, scores_ref, stats_ref):
    slab = own_ref.shape[0]
    qa, wanted = qa_ref[...], wanted_ref[...]
    lines = lax.broadcasted_iota(jnp.int32, (slab, qa.shape[0]), 0)
    parts = []
    for k, ref in enumerate((own_ref, other_ref)):
        part = dot(ref[...], qa, ((1,), (1,))) * scale
        scores_ref[k * slab : (k + 1) * slab, :] = part
        hit = lines == wanted - here_ref[k]
        parts.append((part, jnp.sum(jnp.where(hit, part, 0.0), axis=0, keepdims=True)))
    top = jnp.maximum(*[jnp.max(part, axis=0, keepdims=True) for part, _ in parts])
    mass = sum(jnp.sum(jnp.exp(part - top), axis=0, keepdims=True) for part, _ in parts)
    lse = top + jnp.log(mass)
    picked = parts[0][1] + parts[1][1]
    lines = qa.shape[0] // 128
    for k in range(lines):
        at = slice(k * 128, (k + 1) * 128)
        stats_ref[k : k + 1, :] = lse[:, at]
        stats_ref[lines + k : lines + k + 1, :] = picked[:, at]


def soft_kernel(scale, here_ref, scores_ref, packet_ref, wanted_ref, qa_ref, own_ref, other_ref, dpa_ref, dqa_ref, stats_ref):
    slab, count = own_ref.shape[0], qa_ref.shape[0]
    lines = count // 128
    packet = packet_ref[...]
    each = packet[:, :lines]
    top = jnp.max(each, axis=0)
    lse = top + jnp.log(jnp.sum(jnp.exp(each - top[None]), axis=0))
    stats_ref[...] = lse - jnp.sum(packet[:, lines:], axis=0)
    row = jnp.concatenate([lse[k : k + 1] for k in range(lines)], axis=1)
    wanted = wanted_ref[...]
    rank = lax.broadcasted_iota(jnp.int32, (slab, count), 0)
    dqa = None
    for k, ref in enumerate((own_ref, other_ref)):
        at = slice(k * slab, (k + 1) * slab)
        probs = jnp.exp(scores_ref[at, :] - row)
        hit = (rank == wanted - here_ref[k]).astype(F32)
        dscores = ((probs - hit) * scale).astype(BF16)
        dpa_ref[at, :] = dot(dscores, qa_ref[...], ((1,), (0,))).astype(BF16)
        part = dot(dscores, ref[...], ((0,), (0,)))
        dqa = part if dqa is None else dqa + part
    dqa_ref[...] = dqa.astype(BF16)


def pieces(where_ref, ref, to_ref, away, sems):
    piece = ref.shape[0] // (SIDE * SIDE)
    place = lax.rem(where_ref[1] + away, SIDE)
    copies = []
    for j in range(SIDE):
        index = jnp.where(where_ref[0] == 0, place * SIDE + j, j * SIDE + place)
        rows = pl.ds(pl.multiple_of(index * piece, piece), piece)
        to = to_ref.at[j * piece : (j + 1) * piece]
        copies.append(pltpu.make_async_copy(ref.at[rows], to, sems.at[j]))
    return copies


def grad_first_kernel(
    where_ref, kept_ref, got_ref, mine_ref, theirs_ref, out_ref, sum_ref,
    left_ref, mine_held, sems, dpa_sems,
):
    slab = kept_ref.shape[1]
    batches = []
    for k, ref in enumerate((kept_ref, got_ref)):
        ours = slice(k * slab, (k + 1) * slab)
        batches.append(
            [
                pltpu.make_async_copy(mine_ref.at[ours], mine_held.at[ours], dpa_sems.at[k]),
                *pieces(where_ref, ref, left_ref.at[k], HOPS[0], sems.at[k]),
            ]
        )
        for copy in batches[-1]:
            copy.start()
    block = None
    for k in range(2):
        ours, yours = slice(k * slab, (k + 1) * slab), slice((1 - k) * slab, (2 - k) * slab)
        for copy in batches[k]:
            copy.wait()
        both = mine_held[ours, :] + theirs_ref[yours, :]
        sum_ref[ours, :] = both
        part = dot(left_ref[k], both, ((1,), (0,)))
        block = part if block is None else block + part
    out_ref[...] = block.astype(BF16)


def grad_second_kernel(where_ref, kept_ref, got_ref, sum_ref, *refs):
    *outs, left_ref, sems = refs
    slab = kept_ref.shape[1]
    copies = []
    for n, away in enumerate((*HOPS[1:], 0)):
        copies.append(
            [
                *pieces(where_ref, kept_ref, left_ref.at[0, n], away, sems.at[0, n]),
                *pieces(where_ref, got_ref, left_ref.at[1, n], away, sems.at[1, n]),
            ]
        )
        for copy in copies[-1]:
            copy.start()
    for n, out in enumerate(outs):
        for copy in copies[n]:
            copy.wait()
        block = dot(left_ref[0, n], sum_ref[:slab, :], ((1,), (0,)))
        block += dot(left_ref[1, n], sum_ref[slab:, :], ((1,), (0,)))
        out[...] = block.astype(BF16)


def query_grad_kernel(none_ref, adapter_ref, dqa_ref, out_ref, held_ref, made_ref, sems, out_sem):
    parts = sems.shape[0]
    depth = adapter_ref.shape[0] // parts
    copies = []
    for k in range(parts):
        rows = slice(k * depth, (k + 1) * depth)
        copies.append(pltpu.make_async_copy(adapter_ref.at[rows], held_ref.at[rows], sems.at[k]))
        copies[-1].start()
    for k in range(parts):
        rows = slice(k * depth, (k + 1) * depth)
        copies[k].wait()
        made_ref[:, rows] = dot(dqa_ref[...], held_ref[rows, :], ((1,), (1,))).astype(BF16)
    copy = pltpu.make_async_copy(made_ref, out_ref, out_sem)
    copy.start()
    copy.wait()


def join_kernel(none_ref, own_ref, far_ref, next_ref, last_ref, line_ref, out_ref):
    size = own_ref.shape[0]
    part = dot(line_ref[:, :size], line_ref[:, size:], ((0,), (0,)))
    for ref in (own_ref, far_ref, next_ref, last_ref):
        part += ref[...].astype(F32)
    out_ref[...] = part.astype(BF16)


def line_block(x, which, core):
    cut = x.reshape(x.shape[0], SIDE, SIDE, -1)
    low = lax.dynamic_index_in_dim(cut, which % SIDE, 1, keepdims=False)
    high = lax.dynamic_index_in_dim(cut, which % SIDE, 2, keepdims=False)
    return jnp.where(core == 0, low, high).reshape(x.shape[0], -1)


def per_device(queries, passages, adapter, positives):
    width = adapter.shape[1]
    scale = width ** (-0.5)
    din = adapter.shape[0]
    own_rows, slab_rows = queries.shape[0], passages.shape[0]
    chips = lax.axis_size(CHIP)
    half = chips * own_rows
    chip, core = lax.axis_index(CHIP), lax.axis_index(CORE)
    here = chip * 2 + core
    place = [lax.axis_index(axis) for axis in CHIP]
    stop = jnp.where(core == 0, place[LINE[0]], place[LINE[1]])

    parts = 4
    far = pl.BlockSpec(memory_space=pltpu.HBM)
    dma = pltpu.SemaphoreType.DMA
    local_qa = dot(queries, adapter, ((1,), (0,))).astype(BF16)
    qa = exchanged(jnp.broadcast_to(local_qa[None], (chips, own_rows, width)))
    qa = qa.reshape(half, width)
    pa, kept, given, kept_queries, given_queries = kernel_call(
        main_kernel,
        [
            ((slab_rows, width), BF16),
            ((din // 2, slab_rows), BF16, far),
            ((din // 2, slab_rows), BF16, far),
            ((own_rows, din // 2), BF16),
            ((own_rows, din // 2), BF16),
        ],
        core.reshape(1),
        [(passages, far), (adapter, far), queries],
        scratch=[
            pltpu.VMEM((slab_rows, din), BF16),
            pltpu.VMEM((din, width), BF16),
            pltpu.VMEM((2, din // 2, slab_rows), BF16),
            pltpu.VMEM((slab_rows, width), F32),
            dma((2, parts)),
            dma((2, parts)),
        ],
        limit=28,
    )
    pa_other = to_partner(pa)
    got = to_partner(given)
    got_queries = to_partner(given_queries)

    starts = jnp.stack([here * slab_rows, (here ^ 1) * slab_rows])
    wanted = lax.dynamic_index_in_dim(
        positives.reshape(chips, 2, own_rows), core, 1, keepdims=False
    ).reshape(1, half)
    lines = half // 128
    scores, stats = kernel_call(
        functools.partial(score_kernel, scale),
        [((2 * slab_rows, half), F32), ((2 * lines, 128), F32)],
        starts,
        [qa, pa, pa_other, wanted],
    )
    packet = jnp.broadcast_to(stats[None], (chips, *stats.shape))
    packet = exchanged(packet)
    dpa, dqa, losses = kernel_call(
        functools.partial(soft_kernel, scale),
        [((2 * slab_rows, width), BF16), ((half, width), BF16), ((lines, 128), F32)],
        starts,
        [scores, packet, wanted, qa, pa, pa_other],
    )
    dpa_got = to_partner(dpa)
    dqa = dqa.reshape(chips, own_rows, width)
    dqa_own = exchanged(dqa)
    dqa_own = jnp.sum(dqa_own.astype(F32), axis=0).astype(BF16)
    dqa_own, losses, kept_queries, got_queries = lax.optimization_barrier(
        (dqa_own, losses, kept_queries, got_queries)
    )
    got_dqa = to_partner(dqa_own)
    losses = lax.dynamic_slice_in_dim(losses.reshape(half), chip * own_rows, own_rows, 0)
    chip_queries = jnp.concatenate([kept_queries, got_queries], axis=0)
    blocks = [line_block(chip_queries, stop + hops, core) for hops in (*HOPS, 0)]
    got_dqa, losses, blocks = lax.optimization_barrier((got_dqa, losses, blocks))
    chip_dqa = jnp.concatenate([dqa_own, got_dqa], axis=0)
    loads = [jnp.concatenate([x, chip_dqa], axis=1) for x in blocks]
    line = [lax.ppermute(x, ALL, shift(hops)) for x, hops in zip(loads, HOPS)]
    line = jnp.concatenate([loads[-1], *line], axis=0)

    block = (din // 2 // SIDE, width)

    where = jnp.stack([core, stop])
    first, dpa_sum = kernel_call(
        grad_first_kernel,
        [(block, BF16), (dpa.shape, BF16)],
        where,
        [(kept, far), (got, far), (dpa, far), dpa_got],
        scratch=[
            pltpu.VMEM((2, block[0], slab_rows), BF16),
            pltpu.VMEM(dpa.shape, BF16),
            dma((2, SIDE)),
            dma((2,)),
        ],
    )
    sent = [lax.ppermute(first, ALL, shift(HOPS[0]))]
    *last, own = kernel_call(
        grad_second_kernel,
        [(block, BF16)] * 3,
        where,
        [(kept, far), (got, far), dpa_sum],
        scratch=[pltpu.VMEM((2, 3, block[0], slab_rows), BF16), dma((2, 3, SIDE))],
    )
    sent += [lax.ppermute(x, ALL, shift(hops)) for x, hops in zip(last, HOPS[1:])]
    (query_grad,) = kernel_call(
        query_grad_kernel,
        [((own_rows, din), BF16, far)],
        jnp.zeros((1,), jnp.int32),
        [(adapter, far), dqa_own],
        scratch=[
            pltpu.VMEM(adapter.shape, BF16),
            pltpu.VMEM((own_rows, din), BF16),
            dma((parts,)),
            dma,
        ],
    )
    line, query_grad = lax.optimization_barrier((line, query_grad))
    (grad,) = kernel_call(
        join_kernel, [(block, BF16)], jnp.zeros((1,), jnp.int32), [own, *sent, line]
    )
    spread = lax.all_to_all(
        grad.reshape(SIDE * SIDE, -1, width), ALL, 0, 0, axis_index_groups=planes(), tiled=True
    )
    grad = jnp.sum(spread.astype(F32), axis=0)

    return (grad, query_grad, losses)


def solution(mesh):
    torus = Mesh(mesh.devices.reshape(mesh.shape["row"], SIDE, SIDE, 2), ALL)
    rows = P(ALL, None)
    return jax.shard_map(
        per_device,
        mesh=torus,
        in_specs=(rows, rows, P(), P()),
        out_specs=(rows, rows, P(ALL)),
        check_vma=False,
    )
```

```python
import functools
import itertools

import jax
import jax.numpy as jnp
from jax import lax
from jax.experimental import pallas as pl
from jax.experimental.pallas import tpu as pltpu
from jax.sharding import Mesh
from jax.sharding import PartitionSpec as P

CHIP = ("row", "col_0", "col_1")
CORE = "col_2"
ALL = (*CHIP, CORE)
SIDE = 4
SWAP = [(0, 1), (1, 0)]
HOPS = (2, 1, 3)
LINE = (0, 1)
F32 = jnp.float32
BF16 = jnp.bfloat16


def dot(left, right, dims):
    return lax.dot_general(left, right, (dims, ((), ())), preferred_element_type=F32)


def to_partner(x):
    return lax.ppermute(x, CORE, SWAP)


def exchanged(blocks):
    return lax.all_to_all(blocks, CHIP, split_axis=0, concat_axis=0, tiled=True)


def number(place, core):
    return ((place[0] * SIDE + place[1]) * SIDE + place[2]) * 2 + core


def shift(hops):
    pairs = []
    for *place, core in itertools.product(range(SIDE), range(SIDE), range(SIDE), range(2)):
        there = list(place)
        axis = LINE[core]
        there[axis] = (there[axis] + hops) % SIDE
        pairs.append((number(place, core), number(there, core)))
    return pairs


def planes():
    side = range(SIDE)
    return [
        [number((z, x, y), 0) for x in side for y in side] for z in side
    ] + [[number((z, x, y), 1) for z in side for y in side] for x in side]


def kernel_call(body, outs, scalars, ins, *, grid=(), scratch=(), limit=16):
    room = pl.BlockSpec(memory_space=pltpu.VMEM)
    arrays, in_specs = [], []
    for entry in ins:
        array, spec = entry if isinstance(entry, tuple) else (entry, room)
        place = pltpu.VMEM if spec is room else pltpu.HBM
        arrays.append(pltpu.with_memory_space_constraint(array, place))
        in_specs.append(spec)
    shapes, out_specs = [], []
    for shape, dtype, *spec in outs:
        shapes.append((pltpu.HBM if spec else pltpu.VMEM)(shape, dtype))
        out_specs.append(spec[0] if spec else room)
    return pl.pallas_call(
        body,
        grid_spec=pltpu.PrefetchScalarGridSpec(
            num_scalar_prefetch=1,
            grid=grid,
            in_specs=in_specs,
            out_specs=out_specs,
            scratch_shapes=list(scratch),
        ),
        out_shape=shapes,
        compiler_params=pltpu.CompilerParams(vmem_limit_bytes=limit << 20),
    )(scalars, *arrays)


def main_kernel(
    core_ref, passages_ref, adapter_ref, queries_ref,
    pa_ref, kept_ref, given_ref, kept_q_ref, given_q_ref,
    slab_ref, held_ref, turned_ref, acc_ref, in_sems, out_sems,
):
    low = core_ref[0] == 0
    parts = in_sems.shape[1]
    span = slab_ref.shape[1] // parts
    lanes, run = 128, 32
    arrivals, leaving = [], []
    for k in range(parts):
        at = slice(k * span, (k + 1) * span)
        arrivals.append(
            (
                pltpu.make_async_copy(passages_ref.at[:, at], slab_ref.at[:, at], in_sems.at[0, k]),
                pltpu.make_async_copy(adapter_ref.at[at], held_ref.at[at], in_sems.at[1, k]),
            )
        )
    for copy in itertools.chain(*arrivals):
        copy.start()
    line = lax.broadcasted_iota(jnp.int32, (2 * lanes, lanes), 0)
    lane = lax.broadcasted_iota(jnp.int32, (2 * lanes, lanes), 1)
    source = lane // run * (2 * run) + lane % run
    mine = core_ref[0] * run
    pick = (line == source + mine).astype(BF16)
    leave = (line == source + run - mine).astype(BF16)
    for tile in range(queries_ref.shape[1] // (2 * lanes)):
        here = queries_ref[:, tile * 2 * lanes : (tile + 1) * 2 * lanes]
        to = slice(tile * lanes, (tile + 1) * lanes)
        kept_q_ref[:, to] = dot(here, pick, ((1,), (0,))).astype(BF16)
        given_q_ref[:, to] = dot(here, leave, ((1,), (0,))).astype(BF16)
    unit = (
        lax.broadcasted_iota(jnp.int32, (lanes, lanes), 0)
        == lax.broadcasted_iota(jnp.int32, (lanes, lanes), 1)
    ).astype(BF16)
    for k in range(parts):
        at = slice(k * span, (k + 1) * span)
        arrivals[k][0].wait()
        for tile in range(k * span // lanes, (k + 1) * span // lanes):
            here = slab_ref[:, tile * lanes : (tile + 1) * lanes]
            turned = dot(unit, here, ((1,), (1,))).astype(BF16)
            for part in range(2):
                first = turned[2 * part * run : (2 * part + 1) * run]
                second = turned[(2 * part + 1) * run : (2 * part + 2) * run]
                to = slice((2 * tile + part) * run, (2 * tile + part + 1) * run)
                turned_ref[0, to, :] = jnp.where(low, first, second)
                turned_ref[1, to, :] = jnp.where(low, second, first)
        rows = slice(k * span // 2, (k + 1) * span // 2)
        for which, ref in enumerate((kept_ref, given_ref)):
            copy = pltpu.make_async_copy(
                turned_ref.at[which, rows], ref.at[rows], out_sems.at[which, k]
            )
            copy.start()
            leaving.append(copy)
        arrivals[k][1].wait()
        part = dot(slab_ref[:, at], held_ref[at, :], ((1,), (0,)))
        if k == 0:
            acc_ref[...] = part
        elif k < parts - 1:
            acc_ref[...] += part
        else:
            pa_ref[...] = (acc_ref[...] + part).astype(BF16)
    for copy in leaving:
        copy.wait()


def score_kernel(scale, here_ref, qa_ref, own_ref, other_ref, wanted_ref, scores_ref, stats_ref):
    slab = own_ref.shape[0]
    qa, wanted = qa_ref[...], wanted_ref[...]
    lines = lax.broadcasted_iota(jnp.int32, (slab, qa.shape[0]), 0)
    parts = []
    for k, ref in enumerate((own_ref, other_ref)):
        part = dot(ref[...], qa, ((1,), (1,))) * scale
        scores_ref[k * slab : (k + 1) * slab, :] = part
        hit = lines == wanted - here_ref[k]
        parts.append((part, jnp.sum(jnp.where(hit, part, 0.0), axis=0, keepdims=True)))
    top = jnp.maximum(*[jnp.max(part, axis=0, keepdims=True) for part, _ in parts])
    mass = sum(jnp.sum(jnp.exp(part - top), axis=0, keepdims=True) for part, _ in parts)
    lse = top + jnp.log(mass)
    picked = parts[0][1] + parts[1][1]
    lines = qa.shape[0] // 128
    for k in range(lines):
        at = slice(k * 128, (k + 1) * 128)
        stats_ref[k : k + 1, :] = lse[:, at]
        stats_ref[lines + k : lines + k + 1, :] = picked[:, at]


def soft_kernel(scale, here_ref, scores_ref, packet_ref, wanted_ref, qa_ref, own_ref, other_ref, dpa_ref, dqa_ref, stats_ref):
    slab, count = own_ref.shape[0], qa_ref.shape[0]
    lines = count // 128
    packet = packet_ref[...]
    each = packet[:, :lines]
    top = jnp.max(each, axis=0)
    lse = top + jnp.log(jnp.sum(jnp.exp(each - top[None]), axis=0))
    stats_ref[...] = lse - jnp.sum(packet[:, lines:], axis=0)
    row = jnp.concatenate([lse[k : k + 1] for k in range(lines)], axis=1)
    wanted = wanted_ref[...]
    rank = lax.broadcasted_iota(jnp.int32, (slab, count), 0)
    dqa = None
    for k, ref in enumerate((own_ref, other_ref)):
        at = slice(k * slab, (k + 1) * slab)
        probs = jnp.exp(scores_ref[at, :] - row)
        hit = (rank == wanted - here_ref[k]).astype(F32)
        dscores = ((probs - hit) * scale).astype(BF16)
        dpa_ref[at, :] = dot(dscores, qa_ref[...], ((1,), (0,))).astype(BF16)
        part = dot(dscores, ref[...], ((0,), (0,)))
        dqa = part if dqa is None else dqa + part
    dqa_ref[...] = dqa.astype(BF16)


def pieces(where_ref, ref, to_ref, away, sems):
    piece = ref.shape[0] // (SIDE * SIDE)
    place = lax.rem(where_ref[1] + away, SIDE)
    copies = []
    for j in range(SIDE):
        index = jnp.where(where_ref[0] == 0, place * SIDE + j, j * SIDE + place)
        rows = pl.ds(pl.multiple_of(index * piece, piece), piece)
        to = to_ref.at[j * piece : (j + 1) * piece]
        copies.append(pltpu.make_async_copy(ref.at[rows], to, sems.at[j]))
    return copies


def grad_first_kernel(
    where_ref, kept_ref, got_ref, mine_ref, theirs_ref, up_ref, down_ref, sum_ref,
    left_ref, mine_held, sems, dpa_sems,
):
    slab = kept_ref.shape[1]
    batches = []
    for k, ref in enumerate((kept_ref, got_ref)):
        ours = slice(k * slab, (k + 1) * slab)
        batches.append(
            [
                pltpu.make_async_copy(mine_ref.at[ours], mine_held.at[ours], dpa_sems.at[k]),
                *pieces(where_ref, ref, left_ref.at[k], HOPS[0], sems.at[k]),
            ]
        )
        for copy in batches[-1]:
            copy.start()
    block = None
    for k in range(2):
        ours, yours = slice(k * slab, (k + 1) * slab), slice((1 - k) * slab, (2 - k) * slab)
        for copy in batches[k]:
            copy.wait()
        both = mine_held[ours, :] + theirs_ref[yours, :]
        sum_ref[ours, :] = both
        part = dot(left_ref[k], both, ((1,), (0,)))
        block = part if block is None else block + part
    size = up_ref.shape[0]
    up_ref[...] = block[:size].astype(BF16)
    down_ref[...] = block[size:].astype(BF16)


def relay_kernel(none_ref, next_ref, last_ref, up_ref, down_ref, next_out, last_out):
    size = up_ref.shape[0]
    top, bottom = slice(0, size), slice(size, 2 * size)
    next_out[top, :] = (next_ref[top, :].astype(F32) + up_ref[...].astype(F32)).astype(BF16)
    next_out[bottom, :] = next_ref[bottom, :]
    last_out[top, :] = last_ref[top, :]
    last_out[bottom, :] = (last_ref[bottom, :].astype(F32) + down_ref[...].astype(F32)).astype(BF16)


def grad_second_kernel(where_ref, kept_ref, got_ref, sum_ref, *refs):
    *outs, left_ref, sems = refs
    slab = kept_ref.shape[1]
    copies = []
    for n, away in enumerate((*HOPS[1:], 0)):
        copies.append(
            [
                *pieces(where_ref, kept_ref, left_ref.at[0, n], away, sems.at[0, n]),
                *pieces(where_ref, got_ref, left_ref.at[1, n], away, sems.at[1, n]),
            ]
        )
        for copy in copies[-1]:
            copy.start()
    for n, out in enumerate(outs):
        for copy in copies[n]:
            copy.wait()
        block = dot(left_ref[0, n], sum_ref[:slab, :], ((1,), (0,)))
        block += dot(left_ref[1, n], sum_ref[slab:, :], ((1,), (0,)))
        out[...] = block.astype(BF16)


def query_grad_kernel(none_ref, adapter_ref, dqa_ref, out_ref, held_ref, made_ref, sems, out_sem):
    parts = sems.shape[0]
    depth = adapter_ref.shape[0] // parts
    copies = []
    for k in range(parts):
        rows = slice(k * depth, (k + 1) * depth)
        copies.append(pltpu.make_async_copy(adapter_ref.at[rows], held_ref.at[rows], sems.at[k]))
        copies[-1].start()
    for k in range(parts):
        rows = slice(k * depth, (k + 1) * depth)
        copies[k].wait()
        made_ref[:, rows] = dot(dqa_ref[...], held_ref[rows, :], ((1,), (1,))).astype(BF16)
    copy = pltpu.make_async_copy(made_ref, out_ref, out_sem)
    copy.start()
    copy.wait()


def join_kernel(none_ref, own_ref, next_ref, last_ref, line_ref, out_ref):
    size = own_ref.shape[0]
    part = dot(line_ref[:, :size], line_ref[:, size:], ((0,), (0,)))
    for ref in (own_ref, next_ref, last_ref):
        part += ref[...].astype(F32)
    out_ref[...] = part.astype(BF16)


def line_block(x, which, core):
    cut = x.reshape(x.shape[0], SIDE, SIDE, -1)
    low = lax.dynamic_index_in_dim(cut, which % SIDE, 1, keepdims=False)
    high = lax.dynamic_index_in_dim(cut, which % SIDE, 2, keepdims=False)
    return jnp.where(core == 0, low, high).reshape(x.shape[0], -1)


def per_device(queries, passages, adapter, positives):
    width = adapter.shape[1]
    scale = width ** (-0.5)
    din = adapter.shape[0]
    own_rows, slab_rows = queries.shape[0], passages.shape[0]
    chips = lax.axis_size(CHIP)
    half = chips * own_rows
    chip, core = lax.axis_index(CHIP), lax.axis_index(CORE)
    here = chip * 2 + core
    place = [lax.axis_index(axis) for axis in CHIP]
    stop = jnp.where(core == 0, place[LINE[0]], place[LINE[1]])

    parts = 4
    far = pl.BlockSpec(memory_space=pltpu.HBM)
    dma = pltpu.SemaphoreType.DMA
    local_qa = dot(queries, adapter, ((1,), (0,))).astype(BF16)
    qa = exchanged(jnp.broadcast_to(local_qa[None], (chips, own_rows, width)))
    qa = qa.reshape(half, width)
    pa, kept, given, kept_queries, given_queries = kernel_call(
        main_kernel,
        [
            ((slab_rows, width), BF16),
            ((din // 2, slab_rows), BF16, far),
            ((din // 2, slab_rows), BF16, far),
            ((own_rows, din // 2), BF16),
            ((own_rows, din // 2), BF16),
        ],
        core.reshape(1),
        [(passages, far), (adapter, far), queries],
        scratch=[
            pltpu.VMEM((slab_rows, din), BF16),
            pltpu.VMEM((din, width), BF16),
            pltpu.VMEM((2, din // 2, slab_rows), BF16),
            pltpu.VMEM((slab_rows, width), F32),
            dma((2, parts)),
            dma((2, parts)),
        ],
        limit=28,
    )
    pa_other = to_partner(pa)
    got = to_partner(given)
    got_queries = to_partner(given_queries)

    starts = jnp.stack([here * slab_rows, (here ^ 1) * slab_rows])
    wanted = lax.dynamic_index_in_dim(
        positives.reshape(chips, 2, own_rows), core, 1, keepdims=False
    ).reshape(1, half)
    lines = half // 128
    scores, stats = kernel_call(
        functools.partial(score_kernel, scale),
        [((2 * slab_rows, half), F32), ((2 * lines, 128), F32)],
        starts,
        [qa, pa, pa_other, wanted],
    )
    packet = jnp.broadcast_to(stats[None], (chips, *stats.shape))
    packet = exchanged(packet)
    dpa, dqa, losses = kernel_call(
        functools.partial(soft_kernel, scale),
        [((2 * slab_rows, width), BF16), ((half, width), BF16), ((lines, 128), F32)],
        starts,
        [scores, packet, wanted, qa, pa, pa_other],
    )
    dpa_got = to_partner(dpa)
    dqa = dqa.reshape(chips, own_rows, width)
    dqa_own = exchanged(dqa)
    block = (din // 2 // SIDE, width)
    half_block = (block[0] // 2, width)

    where = jnp.stack([core, stop])
    up, down, dpa_sum = kernel_call(
        grad_first_kernel,
        [(half_block, BF16)] * 2 + [(dpa.shape, BF16)],
        where,
        [(kept, far), (got, far), (dpa, far), dpa_got],
        scratch=[
            pltpu.VMEM((2, block[0], slab_rows), BF16),
            pltpu.VMEM(dpa.shape, BF16),
            dma((2, SIDE)),
            dma((2,)),
        ],
    )
    up = lax.ppermute(up, ALL, shift(HOPS[1]))
    down = lax.ppermute(down, ALL, shift(HOPS[2]))
    *last, own = kernel_call(
        grad_second_kernel,
        [(block, BF16)] * 3,
        where,
        [(kept, far), (got, far), dpa_sum],
        scratch=[pltpu.VMEM((2, 3, block[0], slab_rows), BF16), dma((2, 3, SIDE))],
    )
    last = kernel_call(
        relay_kernel, [(block, BF16)] * 2, jnp.zeros((1,), jnp.int32), [*last, up, down]
    )
    sent = [lax.ppermute(x, ALL, shift(hops)) for x, hops in zip(last, HOPS[1:])]
    dqa_own, own = lax.optimization_barrier((dqa_own, own))
    dqa_own = jnp.sum(dqa_own.astype(F32), axis=0).astype(BF16)
    dqa_own, losses, kept_queries, got_queries = lax.optimization_barrier(
        (dqa_own, losses, kept_queries, got_queries)
    )
    got_dqa = to_partner(dqa_own)
    losses = lax.dynamic_slice_in_dim(losses.reshape(half), chip * own_rows, own_rows, 0)
    chip_queries = jnp.concatenate([kept_queries, got_queries], axis=0)
    blocks = [line_block(chip_queries, stop + hops, core) for hops in (*HOPS, 0)]
    got_dqa, losses, blocks = lax.optimization_barrier((got_dqa, losses, blocks))
    chip_dqa = jnp.concatenate([dqa_own, got_dqa], axis=0)
    loads = [jnp.concatenate([x, chip_dqa], axis=1) for x in blocks]
    line = [lax.ppermute(x, ALL, shift(hops)) for x, hops in zip(loads, HOPS)]
    line = jnp.concatenate([loads[-1], *line], axis=0)

    (query_grad,) = kernel_call(
        query_grad_kernel,
        [((own_rows, din), BF16, far)],
        jnp.zeros((1,), jnp.int32),
        [(adapter, far), dqa_own],
        scratch=[
            pltpu.VMEM(adapter.shape, BF16),
            pltpu.VMEM((own_rows, din), BF16),
            dma((parts,)),
            dma,
        ],
    )
    line, query_grad = lax.optimization_barrier((line, query_grad))
    (grad,) = kernel_call(
        join_kernel, [(block, BF16)], jnp.zeros((1,), jnp.int32), [own, *sent, line]
    )
    spread = lax.all_to_all(
        grad.reshape(SIDE * SIDE, -1, width), ALL, 0, 0, axis_index_groups=planes(), tiled=True
    )
    grad = jnp.sum(spread.astype(F32), axis=0)

    return (grad, query_grad, losses)


def solution(mesh):
    torus = Mesh(mesh.devices.reshape(mesh.shape["row"], SIDE, SIDE, 2), ALL)
    rows = P(ALL, None)
    return jax.shard_map(
        per_device,
        mesh=torus,
        in_specs=(rows, rows, P(), P()),
        out_specs=(rows, rows, P(ALL)),
        check_vma=False,
    )
```

```python
import functools
import itertools

import jax
import jax.numpy as jnp
from jax import lax
from jax.experimental import pallas as pl
from jax.experimental.pallas import tpu as pltpu
from jax.sharding import Mesh
from jax.sharding import PartitionSpec as P

CHIP = ("row", "col_0", "col_1")
CORE = "col_2"
ALL = (*CHIP, CORE)
SIDE = 4
SWAP = [(0, 1), (1, 0)]
HOPS = (2, 1, 3)
LINE = (0, 1)
F32 = jnp.float32
BF16 = jnp.bfloat16


def dot(left, right, dims):
    return lax.dot_general(left, right, (dims, ((), ())), preferred_element_type=F32)


def to_partner(x):
    return lax.ppermute(x, CORE, SWAP)


def exchanged(blocks):
    return lax.all_to_all(blocks, CHIP, split_axis=0, concat_axis=0, tiled=True)


def number(place, core):
    return ((place[0] * SIDE + place[1]) * SIDE + place[2]) * 2 + core


def shift(hops):
    pairs = []
    for *place, core in itertools.product(range(SIDE), range(SIDE), range(SIDE), range(2)):
        there = list(place)
        axis = LINE[core]
        there[axis] = (there[axis] + hops) % SIDE
        pairs.append((number(place, core), number(there, core)))
    return pairs


def planes():
    side = range(SIDE)
    return [
        [number((z, x, y), 0) for x in side for y in side] for z in side
    ] + [[number((z, x, y), 1) for z in side for y in side] for x in side]


def kernel_call(body, outs, scalars, ins, *, grid=(), scratch=(), limit=16):
    room = pl.BlockSpec(memory_space=pltpu.VMEM)
    arrays, in_specs = [], []
    for entry in ins:
        array, spec = entry if isinstance(entry, tuple) else (entry, room)
        place = pltpu.VMEM if spec is room else pltpu.HBM
        arrays.append(pltpu.with_memory_space_constraint(array, place))
        in_specs.append(spec)
    shapes, out_specs = [], []
    for shape, dtype, *spec in outs:
        shapes.append((pltpu.HBM if spec else pltpu.VMEM)(shape, dtype))
        out_specs.append(spec[0] if spec else room)
    return pl.pallas_call(
        body,
        grid_spec=pltpu.PrefetchScalarGridSpec(
            num_scalar_prefetch=1,
            grid=grid,
            in_specs=in_specs,
            out_specs=out_specs,
            scratch_shapes=list(scratch),
        ),
        out_shape=shapes,
        compiler_params=pltpu.CompilerParams(vmem_limit_bytes=limit << 20),
    )(scalars, *arrays)


def main_kernel(
    core_ref, passages_ref, adapter_ref, queries_ref,
    pa_ref, kept_ref, given_ref, kept_q_ref, given_q_ref,
    slab_ref, held_ref, turned_ref, acc_ref, in_sems, out_sems,
):
    low = core_ref[0] == 0
    parts = in_sems.shape[1]
    span = slab_ref.shape[1] // parts
    lanes, run = 128, 32
    arrivals, leaving = [], []
    for k in range(parts):
        at = slice(k * span, (k + 1) * span)
        arrivals.append(
            (
                pltpu.make_async_copy(passages_ref.at[:, at], slab_ref.at[:, at], in_sems.at[0, k]),
                pltpu.make_async_copy(adapter_ref.at[at], held_ref.at[at], in_sems.at[1, k]),
            )
        )
    for copy in itertools.chain(*arrivals):
        copy.start()
    line = lax.broadcasted_iota(jnp.int32, (2 * lanes, lanes), 0)
    lane = lax.broadcasted_iota(jnp.int32, (2 * lanes, lanes), 1)
    source = lane // run * (2 * run) + lane % run
    mine = core_ref[0] * run
    pick = (line == source + mine).astype(BF16)
    leave = (line == source + run - mine).astype(BF16)
    for tile in range(queries_ref.shape[1] // (2 * lanes)):
        here = queries_ref[:, tile * 2 * lanes : (tile + 1) * 2 * lanes]
        to = slice(tile * lanes, (tile + 1) * lanes)
        kept_q_ref[:, to] = dot(here, pick, ((1,), (0,))).astype(BF16)
        given_q_ref[:, to] = dot(here, leave, ((1,), (0,))).astype(BF16)
    unit = (
        lax.broadcasted_iota(jnp.int32, (lanes, lanes), 0)
        == lax.broadcasted_iota(jnp.int32, (lanes, lanes), 1)
    ).astype(BF16)
    for k in range(parts):
        at = slice(k * span, (k + 1) * span)
        arrivals[k][0].wait()
        for tile in range(k * span // lanes, (k + 1) * span // lanes):
            here = slab_ref[:, tile * lanes : (tile + 1) * lanes]
            turned = dot(unit, here, ((1,), (1,))).astype(BF16)
            for part in range(2):
                first = turned[2 * part * run : (2 * part + 1) * run]
                second = turned[(2 * part + 1) * run : (2 * part + 2) * run]
                to = slice((2 * tile + part) * run, (2 * tile + part + 1) * run)
                turned_ref[0, to, :] = jnp.where(low, first, second)
                turned_ref[1, to, :] = jnp.where(low, second, first)
        rows = slice(k * span // 2, (k + 1) * span // 2)
        for which, ref in enumerate((kept_ref, given_ref)):
            copy = pltpu.make_async_copy(
                turned_ref.at[which, rows], ref.at[rows], out_sems.at[which, k]
            )
            copy.start()
            leaving.append(copy)
        arrivals[k][1].wait()
        part = dot(slab_ref[:, at], held_ref[at, :], ((1,), (0,)))
        if k == 0:
            acc_ref[...] = part
        elif k < parts - 1:
            acc_ref[...] += part
        else:
            pa_ref[...] = (acc_ref[...] + part).astype(BF16)
    for copy in leaving:
        copy.wait()


def score_kernel(scale, here_ref, qa_ref, own_ref, other_ref, wanted_ref, scores_ref, stats_ref):
    slab = own_ref.shape[0]
    qa, wanted = qa_ref[...], wanted_ref[...]
    lines = lax.broadcasted_iota(jnp.int32, (slab, qa.shape[0]), 0)
    parts = []
    for k, ref in enumerate((own_ref, other_ref)):
        part = dot(ref[...], qa, ((1,), (1,))) * scale
        scores_ref[k * slab : (k + 1) * slab, :] = part
        hit = lines == wanted - here_ref[k]
        parts.append((part, jnp.sum(jnp.where(hit, part, 0.0), axis=0, keepdims=True)))
    top = jnp.maximum(*[jnp.max(part, axis=0, keepdims=True) for part, _ in parts])
    mass = sum(jnp.sum(jnp.exp(part - top), axis=0, keepdims=True) for part, _ in parts)
    lse = top + jnp.log(mass)
    picked = parts[0][1] + parts[1][1]
    lines = qa.shape[0] // 128
    for k in range(lines):
        at = slice(k * 128, (k + 1) * 128)
        stats_ref[k : k + 1, :] = lse[:, at]
        stats_ref[lines + k : lines + k + 1, :] = picked[:, at]


def soft_kernel(scale, here_ref, scores_ref, packet_ref, wanted_ref, qa_ref, own_ref, other_ref, dpa_ref, dqa_ref, stats_ref):
    slab, count = own_ref.shape[0], qa_ref.shape[0]
    lines = count // 128
    packet = packet_ref[...]
    each = packet[:, :lines]
    top = jnp.max(each, axis=0)
    lse = top + jnp.log(jnp.sum(jnp.exp(each - top[None]), axis=0))
    stats_ref[...] = lse - jnp.sum(packet[:, lines:], axis=0)
    row = jnp.concatenate([lse[k : k + 1] for k in range(lines)], axis=1)
    wanted = wanted_ref[...]
    rank = lax.broadcasted_iota(jnp.int32, (slab, count), 0)
    dqa = None
    for k, ref in enumerate((own_ref, other_ref)):
        at = slice(k * slab, (k + 1) * slab)
        probs = jnp.exp(scores_ref[at, :] - row)
        hit = (rank == wanted - here_ref[k]).astype(F32)
        dscores = ((probs - hit) * scale).astype(BF16)
        dpa_ref[at, :] = dot(dscores, qa_ref[...], ((1,), (0,))).astype(BF16)
        part = dot(dscores, ref[...], ((0,), (0,)))
        dqa = part if dqa is None else dqa + part
    dqa_ref[...] = dqa.astype(BF16)


def pieces(where_ref, ref, to_ref, away, sems):
    piece = ref.shape[0] // (SIDE * SIDE)
    place = lax.rem(where_ref[1] + away, SIDE)
    copies = []
    for j in range(SIDE):
        index = jnp.where(where_ref[0] == 0, place * SIDE + j, j * SIDE + place)
        rows = pl.ds(pl.multiple_of(index * piece, piece), piece)
        to = to_ref.at[j * piece : (j + 1) * piece]
        copies.append(pltpu.make_async_copy(ref.at[rows], to, sems.at[j]))
    return copies


def grad_first_kernel(
    where_ref, kept_ref, got_ref, mine_ref, theirs_ref, up_ref, down_ref, sum_ref,
    left_ref, mine_held, sems, dpa_sems,
):
    slab = kept_ref.shape[1]
    batches = []
    for k, ref in enumerate((kept_ref, got_ref)):
        ours = slice(k * slab, (k + 1) * slab)
        batches.append(
            [
                pltpu.make_async_copy(mine_ref.at[ours], mine_held.at[ours], dpa_sems.at[k]),
                *pieces(where_ref, ref, left_ref.at[k], HOPS[0], sems.at[k]),
            ]
        )
        for copy in batches[-1]:
            copy.start()
    block = None
    for k in range(2):
        ours, yours = slice(k * slab, (k + 1) * slab), slice((1 - k) * slab, (2 - k) * slab)
        for copy in batches[k]:
            copy.wait()
        both = mine_held[ours, :] + theirs_ref[yours, :]
        sum_ref[ours, :] = both
        part = dot(left_ref[k], both, ((1,), (0,)))
        block = part if block is None else block + part
    size = up_ref.shape[0]
    up_ref[...] = block[:size].astype(BF16)
    down_ref[...] = block[size:].astype(BF16)


def relay_kernel(none_ref, next_ref, last_ref, up_ref, down_ref, next_out, last_out):
    next_out[...] = (next_ref[...].astype(F32) + up_ref[...].astype(F32)).astype(BF16)
    last_out[...] = (last_ref[...].astype(F32) + down_ref[...].astype(F32)).astype(BF16)


def grad_second_kernel(where_ref, kept_ref, got_ref, sum_ref, *refs):
    *halves, own_ref, left_ref, sems = refs
    slab, size = kept_ref.shape[1], halves[0].shape[0]
    copies = []
    for n, away in enumerate((*HOPS[1:], 0)):
        copies.append(
            [
                *pieces(where_ref, kept_ref, left_ref.at[0, n], away, sems.at[0, n]),
                *pieces(where_ref, got_ref, left_ref.at[1, n], away, sems.at[1, n]),
            ]
        )
        for copy in copies[-1]:
            copy.start()
    for n in range(3):
        for copy in copies[n]:
            copy.wait()
        block = dot(left_ref[0, n], sum_ref[:slab, :], ((1,), (0,)))
        block += dot(left_ref[1, n], sum_ref[slab:, :], ((1,), (0,)))
        if n < 2:
            halves[2 * n][...] = block[:size].astype(BF16)
            halves[2 * n + 1][...] = block[size:].astype(BF16)
        else:
            own_ref[...] = block.astype(BF16)


def query_grad_kernel(none_ref, adapter_ref, dqa_ref, out_ref, held_ref, made_ref, sems, out_sem):
    parts = sems.shape[0]
    depth = adapter_ref.shape[0] // parts
    copies = []
    for k in range(parts):
        rows = slice(k * depth, (k + 1) * depth)
        copies.append(pltpu.make_async_copy(adapter_ref.at[rows], held_ref.at[rows], sems.at[k]))
        copies[-1].start()
    for k in range(parts):
        rows = slice(k * depth, (k + 1) * depth)
        copies[k].wait()
        made_ref[:, rows] = dot(dqa_ref[...], held_ref[rows, :], ((1,), (1,))).astype(BF16)
    copy = pltpu.make_async_copy(made_ref, out_ref, out_sem)
    copy.start()
    copy.wait()


def join_kernel(none_ref, own_ref, next_top, next_low, last_top, last_low, line_ref, out_ref):
    size = own_ref.shape[0]
    part = dot(line_ref[:, :size], line_ref[:, size:], ((0,), (0,)))
    for k, pair in enumerate(((next_top, last_top), (next_low, last_low))):
        at = slice(k * size // 2, (k + 1) * size // 2)
        here = part[at] + own_ref[at, :].astype(F32)
        for ref in pair:
            here += ref[...].astype(F32)
        out_ref[at, :] = here.astype(BF16)


def line_block(x, which, core):
    cut = x.reshape(x.shape[0], SIDE, SIDE, -1)
    low = lax.dynamic_index_in_dim(cut, which % SIDE, 1, keepdims=False)
    high = lax.dynamic_index_in_dim(cut, which % SIDE, 2, keepdims=False)
    return jnp.where(core == 0, low, high).reshape(x.shape[0], -1)


def per_device(queries, passages, adapter, positives):
    width = adapter.shape[1]
    scale = width ** (-0.5)
    din = adapter.shape[0]
    own_rows, slab_rows = queries.shape[0], passages.shape[0]
    chips = lax.axis_size(CHIP)
    half = chips * own_rows
    chip, core = lax.axis_index(CHIP), lax.axis_index(CORE)
    here = chip * 2 + core
    place = [lax.axis_index(axis) for axis in CHIP]
    stop = jnp.where(core == 0, place[LINE[0]], place[LINE[1]])

    parts = 4
    far = pl.BlockSpec(memory_space=pltpu.HBM)
    dma = pltpu.SemaphoreType.DMA
    local_qa = dot(queries, adapter, ((1,), (0,))).astype(BF16)
    qa = exchanged(jnp.broadcast_to(local_qa[None], (chips, own_rows, width)))
    qa = qa.reshape(half, width)
    pa, kept, given, kept_queries, given_queries = kernel_call(
        main_kernel,
        [
            ((slab_rows, width), BF16),
            ((din // 2, slab_rows), BF16, far),
            ((din // 2, slab_rows), BF16, far),
            ((own_rows, din // 2), BF16),
            ((own_rows, din // 2), BF16),
        ],
        core.reshape(1),
        [(passages, far), (adapter, far), queries],
        scratch=[
            pltpu.VMEM((slab_rows, din), BF16),
            pltpu.VMEM((din, width), BF16),
            pltpu.VMEM((2, din // 2, slab_rows), BF16),
            pltpu.VMEM((slab_rows, width), F32),
            dma((2, parts)),
            dma((2, parts)),
        ],
        limit=28,
    )
    pa_other = to_partner(pa)
    got = to_partner(given)
    got_queries = to_partner(given_queries)

    starts = jnp.stack([here * slab_rows, (here ^ 1) * slab_rows])
    wanted = lax.dynamic_index_in_dim(
        positives.reshape(chips, 2, own_rows), core, 1, keepdims=False
    ).reshape(1, half)
    lines = half // 128
    scores, stats = kernel_call(
        functools.partial(score_kernel, scale),
        [((2 * slab_rows, half), F32), ((2 * lines, 128), F32)],
        starts,
        [qa, pa, pa_other, wanted],
    )
    packet = jnp.broadcast_to(stats[None], (chips, *stats.shape))
    packet = exchanged(packet)
    dpa, dqa, losses = kernel_call(
        functools.partial(soft_kernel, scale),
        [((2 * slab_rows, width), BF16), ((half, width), BF16), ((lines, 128), F32)],
        starts,
        [scores, packet, wanted, qa, pa, pa_other],
    )
    dpa_got = to_partner(dpa)
    dqa = dqa.reshape(chips, own_rows, width)
    dqa_own = exchanged(dqa)
    block = (din // 2 // SIDE, width)
    half_block = (block[0] // 2, width)

    where = jnp.stack([core, stop])
    up, down, dpa_sum = kernel_call(
        grad_first_kernel,
        [(half_block, BF16)] * 2 + [(dpa.shape, BF16)],
        where,
        [(kept, far), (got, far), (dpa, far), dpa_got],
        scratch=[
            pltpu.VMEM((2, block[0], slab_rows), BF16),
            pltpu.VMEM(dpa.shape, BF16),
            dma((2, SIDE)),
            dma((2,)),
        ],
    )
    up = lax.ppermute(up, ALL, shift(HOPS[1]))
    down = lax.ppermute(down, ALL, shift(HOPS[2]))
    next_top, next_low, last_top, last_low, own = kernel_call(
        grad_second_kernel,
        [(half_block, BF16)] * 4 + [(block, BF16)],
        where,
        [(kept, far), (got, far), dpa_sum],
        scratch=[pltpu.VMEM((2, 3, block[0], slab_rows), BF16), dma((2, 3, SIDE))],
    )
    next_low = lax.ppermute(next_low, ALL, shift(HOPS[1]))
    last_top = lax.ppermute(last_top, ALL, shift(HOPS[2]))
    next_top, last_low = kernel_call(
        relay_kernel,
        [(half_block, BF16)] * 2,
        jnp.zeros((1,), jnp.int32),
        [next_top, last_low, up, down],
    )
    next_top = lax.ppermute(next_top, ALL, shift(HOPS[1]))
    last_low = lax.ppermute(last_low, ALL, shift(HOPS[2]))
    dqa_own, own = lax.optimization_barrier((dqa_own, own))
    dqa_own = jnp.sum(dqa_own.astype(F32), axis=0).astype(BF16)
    dqa_own, kept_queries, got_queries = lax.optimization_barrier(
        (dqa_own, kept_queries, got_queries)
    )
    got_dqa = to_partner(dqa_own)
    chip_queries = jnp.concatenate([kept_queries, got_queries], axis=0)
    blocks = [line_block(chip_queries, stop + hops, core) for hops in (*HOPS, 0)]
    got_dqa, blocks = lax.optimization_barrier((got_dqa, blocks))
    chip_dqa = jnp.concatenate([dqa_own, got_dqa], axis=0)
    loads = [jnp.concatenate([x, chip_dqa], axis=1) for x in blocks]
    line = [lax.ppermute(x, ALL, shift(hops)) for x, hops in zip(loads, HOPS)]
    line = jnp.concatenate([loads[-1], *line], axis=0)

    (grad,) = kernel_call(
        join_kernel,
        [(block, BF16)],
        jnp.zeros((1,), jnp.int32),
        [own, next_top, next_low, last_top, last_low, line],
    )
    spread = lax.all_to_all(
        grad.reshape(SIDE * SIDE, -1, width), ALL, 0, 0, axis_index_groups=planes(), tiled=True
    )
    (query_grad,) = kernel_call(
        query_grad_kernel,
        [((own_rows, din), BF16, far)],
        jnp.zeros((1,), jnp.int32),
        [(adapter, far), dqa_own],
        scratch=[
            pltpu.VMEM(adapter.shape, BF16),
            pltpu.VMEM((own_rows, din), BF16),
            dma((parts,)),
            dma,
        ],
    )
    grad, losses = lax.optimization_barrier((grad, losses))
    losses = lax.dynamic_slice_in_dim(losses.reshape(half), chip * own_rows, own_rows, 0)
    grad = jnp.sum(spread.astype(F32), axis=0)

    return (grad, query_grad, losses)


def solution(mesh):
    torus = Mesh(mesh.devices.reshape(mesh.shape["row"], SIDE, SIDE, 2), ALL)
    rows = P(ALL, None)
    return jax.shard_map(
        per_device,
        mesh=torus,
        in_specs=(rows, rows, P(), P()),
        out_specs=(rows, rows, P(ALL)),
        check_vma=False,
    )
```

```python
import functools
import itertools

import jax
import jax.numpy as jnp
from jax import lax
from jax.experimental import pallas as pl
from jax.experimental.pallas import tpu as pltpu
from jax.sharding import Mesh
from jax.sharding import PartitionSpec as P

CHIP = ("row", "col_0", "col_1")
CORE = "col_2"
ALL = (*CHIP, CORE)
SIDE = 4
SWAP = [(0, 1), (1, 0)]
HOPS = (2, 1, 3)
LINE = (0, 1)
F32 = jnp.float32
BF16 = jnp.bfloat16


def dot(left, right, dims):
    return lax.dot_general(left, right, (dims, ((), ())), preferred_element_type=F32)


def to_partner(x):
    return lax.ppermute(x, CORE, SWAP)


def exchanged(blocks):
    return lax.all_to_all(blocks, CHIP, split_axis=0, concat_axis=0, tiled=True)


def number(place, core):
    return ((place[0] * SIDE + place[1]) * SIDE + place[2]) * 2 + core


def shift(hops):
    pairs = []
    for *place, core in itertools.product(range(SIDE), range(SIDE), range(SIDE), range(2)):
        there = list(place)
        axis = LINE[core]
        there[axis] = (there[axis] + hops) % SIDE
        pairs.append((number(place, core), number(there, core)))
    return pairs


def planes():
    side = range(SIDE)
    return [
        [number((z, x, y), 0) for x in side for y in side] for z in side
    ] + [[number((z, x, y), 1) for z in side for y in side] for x in side]


def kernel_call(body, outs, scalars, ins, *, grid=(), scratch=(), limit=24):
    room = pl.BlockSpec(memory_space=pltpu.VMEM)
    arrays, in_specs = [], []
    for entry in ins:
        array, spec = entry if isinstance(entry, tuple) else (entry, room)
        place = pltpu.VMEM if spec is room else pltpu.HBM
        arrays.append(pltpu.with_memory_space_constraint(array, place))
        in_specs.append(spec)
    shapes, out_specs = [], []
    for shape, dtype, *spec in outs:
        shapes.append((pltpu.HBM if spec else pltpu.VMEM)(shape, dtype))
        out_specs.append(spec[0] if spec else room)
    return pl.pallas_call(
        body,
        grid_spec=pltpu.PrefetchScalarGridSpec(
            num_scalar_prefetch=1,
            grid=grid,
            in_specs=in_specs,
            out_specs=out_specs,
            scratch_shapes=list(scratch),
        ),
        out_shape=shapes,
        compiler_params=pltpu.CompilerParams(vmem_limit_bytes=limit << 20),
    )(scalars, *arrays)


def main_kernel(
    core_ref, passages_ref, adapter_ref, queries_ref,
    pa_ref, kept_ref, given_ref, kept_q_ref, given_q_ref,
    slab_ref, held_ref, turned_ref, acc_ref, in_sems, out_sems,
):
    low = core_ref[0] == 0
    parts = in_sems.shape[1]
    span = slab_ref.shape[1] // parts
    lanes, run = 128, 32
    arrivals, leaving = [], []
    for k in range(parts):
        at = slice(k * span, (k + 1) * span)
        arrivals.append(
            (
                pltpu.make_async_copy(passages_ref.at[:, at], slab_ref.at[:, at], in_sems.at[0, k]),
                pltpu.make_async_copy(adapter_ref.at[at], held_ref.at[at], in_sems.at[1, k]),
            )
        )
    for copy in itertools.chain(*arrivals):
        copy.start()
    line = lax.broadcasted_iota(jnp.int32, (2 * lanes, lanes), 0)
    lane = lax.broadcasted_iota(jnp.int32, (2 * lanes, lanes), 1)
    source = lane // run * (2 * run) + lane % run
    mine = core_ref[0] * run
    pick = (line == source + mine).astype(BF16)
    leave = (line == source + run - mine).astype(BF16)
    for tile in range(queries_ref.shape[1] // (2 * lanes)):
        here = queries_ref[:, tile * 2 * lanes : (tile + 1) * 2 * lanes]
        to = slice(tile * lanes, (tile + 1) * lanes)
        kept_q_ref[:, to] = dot(here, pick, ((1,), (0,))).astype(BF16)
        given_q_ref[:, to] = dot(here, leave, ((1,), (0,))).astype(BF16)
    unit = (
        lax.broadcasted_iota(jnp.int32, (lanes, lanes), 0)
        == lax.broadcasted_iota(jnp.int32, (lanes, lanes), 1)
    ).astype(BF16)
    for k in range(parts):
        at = slice(k * span, (k + 1) * span)
        arrivals[k][0].wait()
        for tile in range(k * span // lanes, (k + 1) * span // lanes):
            here = slab_ref[:, tile * lanes : (tile + 1) * lanes]
            turned = dot(unit, here, ((1,), (1,))).astype(BF16)
            for part in range(2):
                first = turned[2 * part * run : (2 * part + 1) * run]
                second = turned[(2 * part + 1) * run : (2 * part + 2) * run]
                to = slice((2 * tile + part) * run, (2 * tile + part + 1) * run)
                turned_ref[0, to, :] = jnp.where(low, first, second)
                turned_ref[1, to, :] = jnp.where(low, second, first)
        rows = slice(k * span // 2, (k + 1) * span // 2)
        for which, ref in enumerate((kept_ref, given_ref)):
            copy = pltpu.make_async_copy(
                turned_ref.at[which, rows], ref.at[rows], out_sems.at[which, k]
            )
            copy.start()
            leaving.append(copy)
        arrivals[k][1].wait()
        part = dot(slab_ref[:, at], held_ref[at, :], ((1,), (0,)))
        if k == 0:
            acc_ref[...] = part
        elif k < parts - 1:
            acc_ref[...] += part
        else:
            pa_ref[...] = (acc_ref[...] + part).astype(BF16)
    for copy in leaving:
        copy.wait()


def score_kernel(scale, here_ref, qa_ref, own_ref, other_ref, wanted_ref, scores_ref, stats_ref):
    slab = own_ref.shape[0]
    qa, wanted = qa_ref[...], wanted_ref[...]
    lines = lax.broadcasted_iota(jnp.int32, (slab, qa.shape[0]), 0)
    parts = []
    for k, ref in enumerate((own_ref, other_ref)):
        part = dot(ref[...], qa, ((1,), (1,))) * scale
        scores_ref[k * slab : (k + 1) * slab, :] = part
        hit = lines == wanted - here_ref[k]
        parts.append((part, jnp.sum(jnp.where(hit, part, 0.0), axis=0, keepdims=True)))
    top = jnp.maximum(*[jnp.max(part, axis=0, keepdims=True) for part, _ in parts])
    mass = sum(jnp.sum(jnp.exp(part - top), axis=0, keepdims=True) for part, _ in parts)
    lse = top + jnp.log(mass)
    picked = parts[0][1] + parts[1][1]
    lines = qa.shape[0] // 128
    for k in range(lines):
        at = slice(k * 128, (k + 1) * 128)
        stats_ref[k : k + 1, :] = lse[:, at]
        stats_ref[lines + k : lines + k + 1, :] = picked[:, at]


def soft_kernel(scale, here_ref, scores_ref, packet_ref, wanted_ref, qa_ref, own_ref, other_ref, dpa_ref, dqa_ref, stats_ref):
    slab, count = own_ref.shape[0], qa_ref.shape[0]
    lines = count // 128
    packet = packet_ref[...]
    each = packet[:, :lines]
    top = jnp.max(each, axis=0)
    lse = top + jnp.log(jnp.sum(jnp.exp(each - top[None]), axis=0))
    stats_ref[...] = lse - jnp.sum(packet[:, lines:], axis=0)
    row = jnp.concatenate([lse[k : k + 1] for k in range(lines)], axis=1)
    wanted = wanted_ref[...]
    rank = lax.broadcasted_iota(jnp.int32, (slab, count), 0)
    dqa = None
    for k, ref in enumerate((own_ref, other_ref)):
        at = slice(k * slab, (k + 1) * slab)
        probs = jnp.exp(scores_ref[at, :] - row)
        hit = (rank == wanted - here_ref[k]).astype(F32)
        dscores = ((probs - hit) * scale).astype(BF16)
        dpa_ref[at, :] = dot(dscores, qa_ref[...], ((1,), (0,))).astype(BF16)
        part = dot(dscores, ref[...], ((0,), (0,)))
        dqa = part if dqa is None else dqa + part
    dqa_ref[...] = dqa.astype(BF16)


def pieces(where_ref, ref, to_ref, away, sems):
    piece = ref.shape[0] // (SIDE * SIDE)
    place = lax.rem(where_ref[1] + away, SIDE)
    copies = []
    for j in range(SIDE):
        index = jnp.where(where_ref[0] == 0, place * SIDE + j, j * SIDE + place)
        rows = pl.ds(pl.multiple_of(index * piece, piece), piece)
        to = to_ref.at[j * piece : (j + 1) * piece]
        copies.append(pltpu.make_async_copy(ref.at[rows], to, sems.at[j]))
    return copies


def grad_first_kernel(
    where_ref, kept_ref, got_ref, mine_ref, theirs_ref, up_ref, down_ref, sum_ref,
    left_ref, mine_held, sems, dpa_sems,
):
    slab = kept_ref.shape[1]
    batches = []
    for k, ref in enumerate((kept_ref, got_ref)):
        ours = slice(k * slab, (k + 1) * slab)
        batches.append(
            [
                pltpu.make_async_copy(mine_ref.at[ours], mine_held.at[ours], dpa_sems.at[k]),
                *pieces(where_ref, ref, left_ref.at[k], HOPS[0], sems.at[k]),
            ]
        )
        for copy in batches[-1]:
            copy.start()
    block = None
    for k in range(2):
        ours, yours = slice(k * slab, (k + 1) * slab), slice((1 - k) * slab, (2 - k) * slab)
        for copy in batches[k]:
            copy.wait()
        both = mine_held[ours, :] + theirs_ref[yours, :]
        sum_ref[ours, :] = both
        part = dot(left_ref[k], both, ((1,), (0,)))
        block = part if block is None else block + part
    size = up_ref.shape[0]
    up_ref[...] = block[:size].astype(BF16)
    down_ref[...] = block[size:].astype(BF16)


def relay_kernel(none_ref, next_ref, last_ref, up_ref, down_ref, next_out, last_out):
    next_out[...] = next_ref[...] + up_ref[...]
    last_out[...] = last_ref[...] + down_ref[...]


def grad_second_kernel(where_ref, kept_ref, got_ref, sum_ref, *refs):
    *halves, own_ref, left_ref, sems = refs
    slab, size = kept_ref.shape[1], halves[0].shape[0]
    copies = []
    for n, away in enumerate((*HOPS[1:], 0)):
        copies.append(
            [
                *pieces(where_ref, kept_ref, left_ref.at[0, n], away, sems.at[0, n]),
                *pieces(where_ref, got_ref, left_ref.at[1, n], away, sems.at[1, n]),
            ]
        )
        for copy in copies[-1]:
            copy.start()
    for n in range(3):
        for copy in copies[n]:
            copy.wait()
        block = dot(left_ref[0, n], sum_ref[:slab, :], ((1,), (0,)))
        block += dot(left_ref[1, n], sum_ref[slab:, :], ((1,), (0,)))
        if n < 2:
            halves[2 * n][...] = block[:size].astype(BF16)
            halves[2 * n + 1][...] = block[size:].astype(BF16)
        else:
            own_ref[...] = block.astype(BF16)


def query_grad_kernel(none_ref, adapter_ref, dqa_ref, out_ref, held_ref, made_ref, sems, out_sem):
    parts = sems.shape[0]
    depth = adapter_ref.shape[0] // parts
    copies = []
    for k in range(parts):
        rows = slice(k * depth, (k + 1) * depth)
        copies.append(pltpu.make_async_copy(adapter_ref.at[rows], held_ref.at[rows], sems.at[k]))
        copies[-1].start()
    for k in range(parts):
        rows = slice(k * depth, (k + 1) * depth)
        copies[k].wait()
        made_ref[:, rows] = dot(dqa_ref[...], held_ref[rows, :], ((1,), (1,))).astype(BF16)
    copy = pltpu.make_async_copy(made_ref, out_ref, out_sem)
    copy.start()
    copy.wait()


def join_kernel(
    none_ref, own_ref, next_top, next_low, last_top, last_low, line_ref, out_ref, made_ref, sems
):
    size = own_ref.shape[0]
    copies = []
    part = dot(line_ref[:, :size], line_ref[:, size:], ((0,), (0,)))
    for k, pair in enumerate(((next_top, last_top), (next_low, last_low))):
        at = slice(k * size // 2, (k + 1) * size // 2)
        here = part[at] + own_ref[at, :].astype(F32)
        for ref in pair:
            here += ref[...].astype(F32)
        made_ref[at, :] = here.astype(BF16)
        copies.append(pltpu.make_async_copy(made_ref.at[at], out_ref.at[at], sems.at[k]))
        copies[-1].start()
    for copy in copies:
        copy.wait()


def line_block(x, which, core):
    cut = x.reshape(x.shape[0], SIDE, SIDE, -1)
    low = lax.dynamic_index_in_dim(cut, which % SIDE, 1, keepdims=False)
    high = lax.dynamic_index_in_dim(cut, which % SIDE, 2, keepdims=False)
    return jnp.where(core == 0, low, high).reshape(x.shape[0], -1)


def per_device(queries, passages, adapter, positives):
    width = adapter.shape[1]
    scale = width ** (-0.5)
    din = adapter.shape[0]
    own_rows, slab_rows = queries.shape[0], passages.shape[0]
    chips = lax.axis_size(CHIP)
    half = chips * own_rows
    chip, core = lax.axis_index(CHIP), lax.axis_index(CORE)
    here = chip * 2 + core
    place = [lax.axis_index(axis) for axis in CHIP]
    stop = jnp.where(core == 0, place[LINE[0]], place[LINE[1]])

    parts = 4
    far = pl.BlockSpec(memory_space=pltpu.HBM)
    dma = pltpu.SemaphoreType.DMA
    local_qa = dot(queries, adapter, ((1,), (0,))).astype(BF16)
    qa = exchanged(jnp.broadcast_to(local_qa[None], (chips, own_rows, width)))
    qa = qa.reshape(half, width)
    pa, kept, given, kept_queries, given_queries = kernel_call(
        main_kernel,
        [
            ((slab_rows, width), BF16),
            ((din // 2, slab_rows), BF16, far),
            ((din // 2, slab_rows), BF16, far),
            ((own_rows, din // 2), BF16),
            ((own_rows, din // 2), BF16),
        ],
        core.reshape(1),
        [(passages, far), (adapter, far), queries],
        scratch=[
            pltpu.VMEM((slab_rows, din), BF16),
            pltpu.VMEM((din, width), BF16),
            pltpu.VMEM((2, din // 2, slab_rows), BF16),
            pltpu.VMEM((slab_rows, width), F32),
            dma((2, parts)),
            dma((2, parts)),
        ],
        limit=28,
    )
    pa_other = to_partner(pa)
    got = to_partner(given)
    got_queries = to_partner(given_queries)

    starts = jnp.stack([here * slab_rows, (here ^ 1) * slab_rows])
    wanted = lax.dynamic_index_in_dim(
        positives.reshape(chips, 2, own_rows), core, 1, keepdims=False
    ).reshape(1, half)
    lines = half // 128
    scores, stats = kernel_call(
        functools.partial(score_kernel, scale),
        [((2 * slab_rows, half), F32), ((2 * lines, 128), F32)],
        starts,
        [qa, pa, pa_other, wanted],
    )
    packet = jnp.broadcast_to(stats[None], (chips, *stats.shape))
    packet = exchanged(packet)
    dpa, dqa, losses = kernel_call(
        functools.partial(soft_kernel, scale),
        [((2 * slab_rows, width), BF16), ((half, width), BF16), ((lines, 128), F32)],
        starts,
        [scores, packet, wanted, qa, pa, pa_other],
    )
    dpa_got = to_partner(dpa)
    dqa = dqa.reshape(chips, own_rows, width)
    dqa_own = exchanged(dqa)
    block = (din // 2 // SIDE, width)
    half_block = (block[0] // 2, width)

    where = jnp.stack([core, stop])
    up, down, dpa_sum = kernel_call(
        grad_first_kernel,
        [(half_block, BF16)] * 2 + [(dpa.shape, BF16)],
        where,
        [(kept, far), (got, far), (dpa, far), dpa_got],
        scratch=[
            pltpu.VMEM((2, block[0], slab_rows), BF16),
            pltpu.VMEM(dpa.shape, BF16),
            dma((2, SIDE)),
            dma((2,)),
        ],
    )
    up = lax.ppermute(up, ALL, shift(HOPS[1]))
    down = lax.ppermute(down, ALL, shift(HOPS[2]))
    next_top, next_low, last_top, last_low, own = kernel_call(
        grad_second_kernel,
        [(half_block, BF16)] * 4 + [(block, BF16)],
        where,
        [(kept, far), (got, far), dpa_sum],
        scratch=[pltpu.VMEM((2, 3, block[0], slab_rows), BF16), dma((2, 3, SIDE))],
    )
    next_low = lax.ppermute(next_low, ALL, shift(HOPS[1]))
    last_top = lax.ppermute(last_top, ALL, shift(HOPS[2]))
    next_top, last_low = kernel_call(
        relay_kernel,
        [(half_block, BF16)] * 2,
        jnp.zeros((1,), jnp.int32),
        [next_top, last_low, up, down],
    )
    next_top = lax.ppermute(next_top, ALL, shift(HOPS[1]))
    last_low = lax.ppermute(last_low, ALL, shift(HOPS[2]))
    dqa_own, own = lax.optimization_barrier((dqa_own, own))
    dqa_own = jnp.sum(dqa_own.astype(F32), axis=0).astype(BF16)
    dqa_own, kept_queries, got_queries = lax.optimization_barrier(
        (dqa_own, kept_queries, got_queries)
    )
    got_dqa = to_partner(dqa_own)
    chip_queries = jnp.concatenate([kept_queries, got_queries], axis=0)
    blocks = [line_block(chip_queries, stop + hops, core) for hops in (*HOPS, 0)]
    got_dqa, blocks = lax.optimization_barrier((got_dqa, blocks))
    chip_dqa = jnp.concatenate([dqa_own, got_dqa], axis=0)
    loads = [jnp.concatenate([x, chip_dqa], axis=1) for x in blocks]
    line = [lax.ppermute(x, ALL, shift(hops)) for x, hops in zip(loads, HOPS)]
    line = jnp.concatenate([loads[-1], *line], axis=0)

    (grad,) = kernel_call(
        join_kernel,
        [(block, BF16, far)],
        jnp.zeros((1,), jnp.int32),
        [own, next_top, next_low, last_top, last_low, line],
        scratch=[pltpu.VMEM(block, BF16), dma((2,))],
    )
    spread = lax.all_to_all(
        grad.reshape(SIDE * SIDE, -1, width), ALL, 0, 0, axis_index_groups=planes(), tiled=True
    )
    (query_grad,) = kernel_call(
        query_grad_kernel,
        [((own_rows, din), BF16, far)],
        jnp.zeros((1,), jnp.int32),
        [(adapter, far), dqa_own],
        scratch=[
            pltpu.VMEM(adapter.shape, BF16),
            pltpu.VMEM((own_rows, din), BF16),
            dma((parts,)),
            dma,
        ],
    )
    grad, losses = lax.optimization_barrier((grad, losses))
    losses = lax.dynamic_slice_in_dim(losses.reshape(half), chip * own_rows, own_rows, 0)
    grad = jnp.sum(spread.astype(F32), axis=0)

    return (grad, query_grad, losses)


def solution(mesh):
    torus = Mesh(mesh.devices.reshape(mesh.shape["row"], SIDE, SIDE, 2), ALL)
    rows = P(ALL, None)
    return jax.shard_map(
        per_device,
        mesh=torus,
        in_specs=(rows, rows, P(), P()),
        out_specs=(rows, rows, P(ALL)),
        check_vma=False,
    )
```
